32 devices in a mesh: parts: 2 (over x), scene: 4 (over y, core), range: 4 (over z).
Axes of the slice: x: 2, y: 2, z: 4, core: 2. Of those that a mesh axis runs over, the one named last changes fastest.
Arguments:
- secondary: bfloat16 [16, 1056, 2, 1024], P(('parts', 'scene'), None, None, 'range'), parts along dimension 0, may hold values from -6 to 6
- reference_store: bfloat16 [8, 4, 256, 2, 1024], P(('parts', 'scene'), None, None, None, 'range'), parts along dimension 0, may hold values from -6 to 6
- tile_owner: int32 [8], P('parts'), parts along dimension 0, may hold values from 0 to 3
- az_kernel: float32 [64, 8], replicated, may hold values from -2 to 2
- rg_kernel: float32 [64, 8], replicated, may hold values from -2 to 2
- az_offset: int32 [16, 1024], P(('parts', 'scene')), parts along dimension 0, may hold values from -12 to 12
- az_index: int32 [16, 1024], P(('parts', 'scene')), parts along dimension 0, may hold values from 0 to 63
- rg_offset: int32 [16, 1024], P(('parts', 'scene'), 'range'), parts along dimension 0, may hold values from -12 to 12
- rg_index: int32 [16, 1024], P(('parts', 'scene'), 'range'), parts along dimension 0, may hold values from 0 to 63
Outputs:
- reference_pairs: float32 [16, 2, 256, 64], P(('parts', 'scene'), None, None, 'range'), parts along dimension 0
- sequential_pairs: float32 [16, 2, 256, 64], P(('parts', 'scene'), None, None, 'range'), parts along dimension 0
- coherence: float32 [16, 256, 64], P(('parts', 'scene'), None, 'range'), parts along dimension 0
The draws below stay inside these ranges and needn't reach their ends.
There are 2 independent parts, one for each index of `parts`. The reference program is written for one: setup_inputs(seed, part) draws one part's arguments, and reference() takes and returns one part's arrays. A program takes and returns all parts, laid end to end along the dimension named above; an argument that names none is the same for every part. Nothing has to cross between parts.
Inputs may be any that keep to these rules, and one draw needn't show every extreme that they name: `tile_owner`: the scene device holding reference tile s.
All inputs are finite; a program needn't handle non-finite values.
Results may differ from the reference program's by a relative error of at most 0.008.
Values may be sent and summed in bfloat16 or wider, within the bound.
No kernel may reach another device: no remote copies, remote signals or barrier semaphores. Data moves between devices by JAX's collectives and lax.ppermute only.
A program may use at most 128 MiB of HBM per device.

```python
from functools import partial
import jax
import jax.numpy as jnp
from jax import lax

CDEV = 256
TILE = 256
NSTEP = 4
TAPS = 8
NKER = 64
MAXOFF = 12
LOOK_AZ = 4
LOOK_RG = 16
PAD = 16
SCENES = 8
RANGE = 1024
ROWS = 1024
N_SCENE = 4
N_RANGE = 4


def set_ends(result, key, low, top_value):
    place = [jax.random.randint(jax.random.fold_in(key, axis), (), 0, length) for axis, length in enumerate(result.shape)]
    longest = result.shape.index(max(result.shape))
    next_to = place[:longest] + [(place[longest] + 1) % result.shape[longest]] + place[longest + 1:]
    return result.at[tuple(place)].set(low).at[tuple(next_to)].set(top_value)


def block_scale(own_key, shape, shards, smallest, largest):
    loudness, own = 1.0, jax.random.fold_in(own_key, 6)
    for position, parts in shards:
        draws = jnp.exp(jax.random.uniform(jax.random.fold_in(own, position), (parts,), jnp.float32, smallest / len(shards), largest / len(shards)))
        loudness = loudness * jnp.repeat(draws, shape[position] // parts).reshape([-1 if axis == position else 1 for axis in range(len(shape))])
    return loudness


def normal_values(own_key, shape, spread, reach, cuts=(), kind=jnp.bfloat16):
    loudness = block_scale(own_key, shape, cuts, -0.22, 0.18) if cuts else 1.0
    array = jax.random.normal(own_key, shape, jnp.float32) * spread * loudness
    return jnp.minimum(jnp.maximum(array, -reach), reach).astype(kind)


def setup_inputs(seed: int = 0, part: int = 0) -> dict:
    streams_of = jax.random.split(jax.random.key(seed), 10)
    part_keys = jax.random.split(jax.random.fold_in(streams_of[9], part), 10)
    return {
        "secondary": normal_values(part_keys[0], (SCENES, ROWS + 2 * PAD, 2, RANGE), 1.0, 6.0, ((0, 4), (3, 4))),
        "reference_store": normal_values(part_keys[1], (N_SCENE, NSTEP, TILE, 2, RANGE), 1.0, 6.0, ((0, 4), (4, 4))),
        "tile_owner": set_ends(jax.random.randint(part_keys[2], (NSTEP,), 0, N_SCENE), jax.random.fold_in(part_keys[2], 1), 0, N_SCENE - 1).astype(jnp.int32),
        "az_kernel": normal_values(streams_of[3], (NKER, TAPS), 0.35, 2.0, (), jnp.float32),
        "rg_kernel": normal_values(streams_of[4], (NKER, TAPS), 0.35, 2.0, (), jnp.float32),
        "az_offset": set_ends(jax.random.randint(part_keys[5], (SCENES, ROWS), 0 - MAXOFF, MAXOFF + 1), jax.random.fold_in(part_keys[5], 1), 0 - MAXOFF, MAXOFF).astype(jnp.int32),
        "az_index": set_ends(jax.random.randint(part_keys[6], (SCENES, ROWS), 0, NKER), jax.random.fold_in(part_keys[6], 1), 0, NKER - 1).astype(jnp.int32),
        "rg_offset": set_ends(jax.random.randint(part_keys[7], (SCENES, RANGE), 0 - MAXOFF, MAXOFF + 1), jax.random.fold_in(part_keys[7], 1), 0 - MAXOFF, MAXOFF).astype(jnp.int32),
        "rg_index": set_ends(jax.random.randint(part_keys[8], (SCENES, RANGE), 0, NKER), jax.random.fold_in(part_keys[8], 1), 0, NKER - 1).astype(jnp.int32),
    }


eps_power = 1e-06

def band_matrix(tap_values, offsets, margin):
    length = offsets.shape[0]
    row_base = jnp.arange(length, dtype=jnp.int32) + offsets + (margin - 3)
    columns = jnp.arange(length + 2 * margin, dtype=jnp.int32)
    matrix = jnp.zeros((length, length + 2 * margin), jnp.float32)
    for tap_index in range(tap_values.shape[1]):
        matrix = matrix + jnp.where(columns[None, :] == (row_base + tap_index)[:, None], tap_values[:, tap_index:tap_index + 1], 0.0)
    return matrix.astype(jnp.bfloat16)

def multilook(sample):
    scenes, height, breadth = sample.shape
    blocks = sample.reshape(scenes, height // LOOK_AZ, LOOK_AZ, breadth // LOOK_RG, LOOK_RG)
    return lax.optimization_barrier(jnp.mean(blocks, axis=(2, 4)))

def products(reference_tile, current, earlier):
    cur_val = current.astype(jnp.float32)
    cur_re, cur_im = (cur_val[:, :, 0], cur_val[:, :, 1])
    pri_val = earlier.astype(jnp.float32)
    pri_re, pri_im = (pri_val[:, :, 0], pri_val[:, :, 1])
    ref_val = reference_tile.astype(jnp.float32)[None]
    ref_re, ref_im = (ref_val[:, :, 0], ref_val[:, :, 1])
    pair_re = multilook(ref_re * cur_re + ref_im * cur_im)
    pair_im = multilook(ref_im * cur_re - ref_re * cur_im)
    seq_re = multilook(pri_re * cur_re + pri_im * cur_im)
    seq_im = multilook(pri_im * cur_re - pri_re * cur_im)
    power_earlier = multilook(pri_re * pri_re + pri_im * pri_im)
    power_current = multilook(cur_re * cur_re + cur_im * cur_im)
    magnitude = jnp.sqrt(seq_re * seq_re + seq_im * seq_im)
    coherent = magnitude / jnp.sqrt(power_earlier * power_current + eps_power)
    return (jnp.stack([pair_re, pair_im], 1), jnp.stack([seq_re, seq_im], 1), coherent)

def reference(secondary, reference_store, tile_owner, az_kernel, rg_kernel, az_offset, az_index, rg_offset, rg_index):
    banded = jax.vmap(partial(band_matrix, margin=PAD))
    widened = jnp.pad(secondary, ((0, 0), (0, 0), (0, 0), (PAD, PAD)))
    rg_taps = rg_kernel[rg_index]
    pair_parts, seq_parts, coh_parts = ([], [], [])
    for tile_step in range(NSTEP):
        row_start = tile_step * TILE
        reference_tile = lax.dynamic_index_in_dim(reference_store, tile_owner[tile_step], 0, keepdims=False)[tile_step]
        tile_rows = widened[:, row_start:row_start + TILE + 2 * PAD]
        az_taps = az_kernel[az_index[:, row_start:row_start + TILE]]
        az_matrix = banded(az_taps, az_offset[:, row_start:row_start + TILE])
        az_result = jnp.einsum('skq,sqpw->skpw', az_matrix.astype(jnp.float32), tile_rows.astype(jnp.float32)).astype(jnp.bfloat16)
        pieces = []
        for column_block in range(N_RANGE):
            col_start = column_block * CDEV
            rg_matrix = banded(rg_taps[:, col_start:col_start + CDEV], rg_offset[:, col_start:col_start + CDEV])
            window = az_result[..., col_start:col_start + CDEV + 2 * PAD].astype(jnp.float32)
            pieces.append(jnp.einsum('skpw,scw->skpc', window, rg_matrix.astype(jnp.float32)).astype(jnp.bfloat16))
        current = jnp.concatenate(pieces, -1)
        earlier = jnp.concatenate([reference_tile[None], current[:-1]], 0)
        pair_out, seq_out, coh_out = products(reference_tile, current, earlier)
        pair_parts.append(pair_out)
        seq_parts.append(seq_out)
        coh_parts.append(coh_out)
    return (jnp.concatenate(pair_parts, 2), jnp.concatenate(seq_parts, 2), jnp.concatenate(coh_parts, 1))
```

```python
from functools import partial

import jax
import jax.numpy as jnp
from jax import lax
from jax.experimental import pallas as pl
from jax.experimental.pallas import tpu as pltpu
from jax.sharding import PartitionSpec as P

TILE = 256
NSTEP = 4
LOOK_AZ = 4
LOOK_RG = 16

eps_power = 1e-06

BF = jnp.bfloat16
F32 = jnp.float32
OVER_ROWS = (((0,), (0,)), ((), ()))
OVER_LANES = (((1,), (1,)), ((), ()))


def iota(shape, dim):
    return lax.broadcasted_iota(jnp.int32, shape, dim)


def dot(a, b, dims=(((1,), (0,)), ((), ()))):
    return lax.dot_general(a, b, dims, preferred_element_type=F32)


def lane_row(lane, half_rows):
    blocks = half_rows // LOOK_AZ
    inner = lane % half_rows
    return LOOK_AZ * (inner % blocks) + inner // blocks, (lane // half_rows) % 2


def sublane_column(sublane, columns):
    blocks = columns // LOOK_RG
    return LOOK_RG * (sublane % blocks) + sublane // blocks


def taps_and_offsets(kernel_t, index_row, offset_row, spread):
    count = kernel_t.shape[1]
    chosen = (iota((count, index_row.shape[1]), 0) == index_row).astype(F32).astype(BF)
    taps = dot(kernel_t.astype(BF), chosen)
    offsets = jnp.broadcast_to(offset_row.astype(F32), (8, offset_row.shape[1]))
    return dot(jnp.concatenate([taps, offsets], 0).astype(BF), spread)


def split_kernel(core_ref, own_ref, other_ref, own_out, other_out, order_ref, columns_ref):
    half_rows = own_ref.shape[2]
    columns = own_ref.shape[4]

    @pl.when(pl.program_id(0) == 0)
    def _():
        shape = (2 * half_rows, 2 * half_rows)
        row, part = lane_row(iota(shape, 1), half_rows)
        order_ref[...] = (iota(shape, 0) == 2 * row + part).astype(F32).astype(BF)
        shape = (columns, columns)
        columns_ref[...] = (
            (iota(shape, 1) == sublane_column(iota(shape, 0), columns)).astype(F32).astype(BF)
        )

    for source, target in ((other_ref, other_out), (own_ref, own_out)):
        rows = source[0, 0].reshape(2 * half_rows, columns)
        turned = dot(columns_ref[...], rows, OVER_LANES).astype(BF)
        target[0] = dot(turned, order_ref[...]).astype(BF)


def split_halves(reference_store, core):
    _, steps, tile, parts, columns = reference_store.shape
    half = tile // 2
    block = (1, 1, half, parts, columns)
    out_block = (1, columns, parts * half)
    out_shape = jax.ShapeDtypeStruct((steps, columns, parts * half), BF)
    return pl.pallas_call(
        split_kernel,
        grid_spec=pltpu.PrefetchScalarGridSpec(
            num_scalar_prefetch=1,
            grid=(steps,),
            in_specs=[
                pl.BlockSpec(block, lambda s, core: (0, s, core[0], 0, 0)),
                pl.BlockSpec(block, lambda s, core: (0, s, 1 - core[0], 0, 0)),
            ],
            out_specs=[pl.BlockSpec(out_block, lambda s, core: (s, 0, 0))] * 2,
            scratch_shapes=[
                pltpu.VMEM((parts * half, parts * half), BF),
                pltpu.VMEM((columns, columns), BF),
            ],
        ),
        out_shape=[out_shape] * 2,
        name="split_halves",
    )(core, reference_store, reference_store)


def azimuth_kernel(
    margin, steps, x_ref, azk_ref, rgk_ref, azo_ref, azi_ref, rgo_ref, rgi_ref,
    z_ref, head_ref, tail_ref, rg_ref, spread_ref, band_ref,
):
    k, s = pl.program_id(0), pl.program_id(1)
    depth, columns = azo_ref.shape[0], x_ref.shape[3]
    taps = azk_ref.shape[0]
    lanes = spread_ref.shape[1]
    tile = lanes // 2
    half = tile // 2

    @pl.when((k == 0) & (s == 0))
    def _():
        row, _ = lane_row(iota((tile, lanes), 1), half)
        row = row + half * (iota((tile, lanes), 1) // tile)
        spread_ref[...] = (iota((tile, lanes), 0) == row).astype(F32).astype(BF)

    @pl.when(s == 0)
    def _():
        shape = (columns, columns)
        order = (iota(shape, 0) == sublane_column(iota(shape, 1), columns)).astype(F32).astype(BF)
        index_row, offset_row = rgi_ref[0:1], rgo_ref[0:1]
        for other in range(1, depth):
            index_row = jnp.where(k == other, rgi_ref[other : other + 1], index_row)
            offset_row = jnp.where(k == other, rgo_ref[other : other + 1], offset_row)
        both = taps_and_offsets(rgk_ref[...], index_row, offset_row, order)
        column = sublane_column(iota((1, columns), 1), columns)
        base = column + both[taps : taps + 1].astype(jnp.int32) + (margin - 3)
        period = 2 * taps
        sub = iota((period, columns), 0)
        which = (sub - base) & (taps - 1)
        value = jnp.zeros((period, columns), F32)
        for tap in range(taps):
            value = jnp.where(which == tap, both[tap : tap + 1], value)
        for block in range(rg_ref.shape[1] // period):
            place = sub + block * period - base
            inside = (place >= 0) & (place < taps)
            rg_ref[0, block * period : (block + 1) * period] = jnp.where(inside, value, 0.0).astype(BF)

    start = pl.multiple_of(s * tile, tile)
    index_row = azi_ref[0:1, pl.ds(start, tile)]
    offset_row = azo_ref[0:1, pl.ds(start, tile)]
    for other in range(1, depth):
        index_row = jnp.where(k == other, azi_ref[other : other + 1, pl.ds(start, tile)], index_row)
        offset_row = jnp.where(k == other, azo_ref[other : other + 1, pl.ds(start, tile)], offset_row)
    both = taps_and_offsets(azk_ref[...], index_row, offset_row, spread_ref[...])
    lane = iota((1, lanes), 1)
    row, part = lane_row(lane, half)
    base = row + half * (lane // tile) + both[taps : taps + 1].astype(jnp.int32) + (margin - 3)
    period = 2 * taps
    sub = iota((period, lanes), 0)
    which = jnp.where((sub & 1) == part, ((sub >> 1) - base) & (taps - 1), taps)
    value = jnp.zeros((period, lanes), F32)
    for tap in range(taps):
        value = jnp.where(which == tap, both[tap : tap + 1], value)
    home = (base - (sub >> 1) + (taps - 1)) // taps
    for block in range(band_ref.shape[0] // period):
        band_ref[block * period : (block + 1) * period] = jnp.where(home == block, value, 0.0).astype(BF)
    rows = x_ref[0, pl.ds(start, tile + 2 * margin)].reshape(band_ref.shape[0], columns)
    z = dot(rows, band_ref[...], OVER_ROWS).astype(BF)
    z_ref[0, 0] = z
    head_ref[0, 0] = z[:margin]
    tail_ref[0, 0] = z[columns - margin :]


def azimuth(secondary, az_kernel, rg_kernel, az_offset, az_index, rg_offset, rg_index):
    depth, rows, parts, columns = secondary.shape
    margin = (rows - az_offset.shape[1]) // 2
    steps = az_offset.shape[1] // TILE
    lanes = parts * TILE
    whole = lambda a: pl.BlockSpec(a.shape, lambda k, s: (0,) * a.ndim)
    small = (az_kernel.T, rg_kernel.T, az_offset, az_index, rg_offset, rg_index)
    edge = jax.ShapeDtypeStruct((depth, steps, margin, lanes), BF)
    edge_spec = pl.BlockSpec((1, 1, margin, lanes), lambda k, s: (k, s, 0, 0))
    return pl.pallas_call(
        partial(azimuth_kernel, margin, steps),
        grid=(depth, steps),
        in_specs=[pl.BlockSpec((1, rows, parts, columns), lambda k, s: (k, 0, 0, 0))]
        + [whole(a) for a in small],
        out_specs=[
            pl.BlockSpec((1, 1, columns, lanes), lambda k, s: (k, s, 0, 0)),
            edge_spec,
            edge_spec,
            pl.BlockSpec((1, columns + 2 * margin, columns), lambda k, s: (k, 0, 0)),
        ],
        out_shape=[
            jax.ShapeDtypeStruct((depth, steps, columns, lanes), BF),
            edge,
            edge,
            jax.ShapeDtypeStruct((depth, columns + 2 * margin, columns), BF),
        ],
        scratch_shapes=[
            pltpu.VMEM((TILE, lanes), BF),
            pltpu.VMEM((parts * (TILE + 2 * margin), lanes), BF),
        ],
        name="azimuth",
    )(secondary, *small)


def halves(block):
    width = block.shape[1] // 2
    wide = block.astype(F32)
    return wide[:, :width], wide[:, width:]


def looks(value):
    blocks = value.shape[0] // LOOK_RG
    total = value[:blocks]
    for look in range(1, LOOK_RG):
        total = total + value[look * blocks : (look + 1) * blocks]
    width = value.shape[1]
    shift = width // 2
    while shift >= width // LOOK_AZ:
        total = total + pltpu.roll(total, shift, 1)
        shift //= 2
    return total * (1.0 / (LOOK_AZ * LOOK_RG))


def pair(first, second):
    a_re, a_im = first
    b_re, b_im = second
    return looks(a_re * b_re + a_im * b_im), looks(a_im * b_re - a_re * b_im)


def power(first):
    re, im = first
    return looks(re * re + im * im)


def store(ref, lead, position, value):
    blocks = value.shape[1] // LOOK_AZ
    here = iota(value.shape, 1) // blocks >= position
    ref[lead] = jnp.where(here, value, ref[lead])


def range_kernel(z_ref, head_ref, tail_ref, rg_ref, *outs):
    depth = z_ref.shape[0]
    cur_refs, (seq_ref, pow_ref) = outs[:depth], outs[depth:]
    s = pl.program_id(0)
    before = None
    for k in range(depth):
        wide = jnp.concatenate([head_ref[k, 0], z_ref[k, 0], tail_ref[k, 0]], 0)
        out = dot(rg_ref[k], wide, OVER_ROWS).astype(BF)
        width = out.shape[1] // 2
        now = []
        for half in range(2):
            part = out[:, half * width : (half + 1) * width]
            cur_refs[k][0, half] = part
            now.append(halves(part))
            store(pow_ref, k, 2 * s + half, power(now[half]))
            if k:
                re, im = pair(before[half], now[half])
                store(seq_ref, (k - 1, 0), 2 * s + half, re)
                store(seq_ref, (k - 1, 1), 2 * s + half, im)
        before = now


def small_spec(shape):
    return pl.BlockSpec(shape, lambda *_: (0,) * len(shape))


def range_resample(z, head, tail, rg, first, count):
    depth, _, columns, lanes = z.shape
    margin = head.shape[2]
    at = lambda s: (0, first + s, 0, 0)
    blocks = columns // LOOK_RG
    width = lanes // 4
    cur_block = (1, 2, columns, lanes // 2)
    small = [(max(depth - 1, 1), 2, blocks, width), (depth, blocks, width)]
    return pl.pallas_call(
        range_kernel,
        grid=(count,),
        in_specs=[
            pl.BlockSpec((depth, 1, columns, lanes), at),
            pl.BlockSpec((depth, 1, margin, lanes), at),
            pl.BlockSpec((depth, 1, margin, lanes), at),
            small_spec(rg.shape),
        ],
        out_specs=[pl.BlockSpec(cur_block, lambda s: (s, 0, 0, 0))] * depth
        + [small_spec(shape) for shape in small],
        out_shape=[jax.ShapeDtypeStruct((count, *cur_block[1:]), BF)] * depth
        + [jax.ShapeDtypeStruct(shape, F32) for shape in small],
        name="range_resample",
    )(z, head, tail, rg)


def reference_kernel(core_ref, own_ref, mate_ref, *refs):
    depth = len(refs) - 2
    cur_refs, (pair_ref, pow_ref) = refs[:depth], refs[depth:]
    s, half = pl.program_id(0), pl.program_id(1)
    tile = halves(jnp.where(half == core_ref[0], own_ref[0], mate_ref[0]))
    position = 2 * s + half
    store(pow_ref, slice(None), position, power(tile))
    for k in range(depth):
        re, im = pair(tile, halves(cur_refs[k][0, 0]))
        store(pair_ref, (k, 0), position, re)
        store(pair_ref, (k, 1), position, im)


def reference_products(core, own, mate, currents):
    count, columns, width = own.shape
    depth = len(currents)
    blocks = columns // LOOK_RG
    lanes = width // 2
    tile_spec = pl.BlockSpec((1, columns, width), lambda s, h, core: (s, 0, 0))
    cur_spec = pl.BlockSpec((1, 1, columns, width), lambda s, h, core: (s, h, 0, 0))
    shapes = [(depth, 2, blocks, lanes), (blocks, lanes)]
    return pl.pallas_call(
        reference_kernel,
        grid_spec=pltpu.PrefetchScalarGridSpec(
            num_scalar_prefetch=1,
            grid=(count, 2),
            in_specs=[tile_spec] * 2 + [cur_spec] * depth,
            out_specs=[small_spec(shape) for shape in shapes],
        ),
        out_shape=[jax.ShapeDtypeStruct(shape, F32) for shape in shapes],
        name="reference_products",
    )(core, own, mate, *currents)


def leading_kernel(handed_ref, cur_ref, pair_ref, pow_ref):
    s = pl.program_id(0)
    for half in range(2):
        lead = halves(handed_ref[0, half])
        re, im = pair(lead, halves(cur_ref[0, half]))
        store(pow_ref, slice(None), 2 * s + half, power(lead))
        store(pair_ref, 0, 2 * s + half, re)
        store(pair_ref, 1, 2 * s + half, im)


def leading_products(handed, current):
    count, _, columns, width = handed.shape
    blocks = columns // LOOK_RG
    lanes = width // 2
    spec = pl.BlockSpec((1, 2, columns, width), lambda s: (s, 0, 0, 0))
    shapes = [(2, blocks, lanes), (blocks, lanes)]
    return pl.pallas_call(
        leading_kernel,
        grid=(count,),
        in_specs=[spec] * 2,
        out_specs=[small_spec(shape) for shape in shapes],
        out_shape=[jax.ShapeDtypeStruct(shape, F32) for shape in shapes],
        name="leading_products",
    )(handed, current)


def finish_kernel(chunks, head_ref, *refs):
    inputs, (ref_out, seq_out, coh_out) = refs[: 6 * chunks], refs[6 * chunks :]
    depth = ref_out.shape[0]
    at_head = head_ref[0] == 1
    lanes = inputs[1].shape[-1]
    for chunk in range(chunks):
        pairs, pair_pow, lead, lead_pow, seq, powers = inputs[6 * chunk : 6 * chunk + 6]
        rows = slice(chunk * lanes, (chunk + 1) * lanes)
        earlier = jnp.where(at_head, pair_pow[...], lead_pow[...])
        for k in range(depth):
            if k:
                re, im = seq[k - 1, 0], seq[k - 1, 1]
            else:
                re = jnp.where(at_head, pairs[0, 0], lead[0])
                im = jnp.where(at_head, pairs[0, 1], lead[1])
            now = powers[k]
            coherent = jnp.sqrt(re * re + im * im) / jnp.sqrt(earlier * now + eps_power)
            earlier = now
            ref_out[k, 0, rows] = pairs[k, 0].T
            ref_out[k, 1, rows] = pairs[k, 1].T
            seq_out[k, 0, rows] = re.T
            seq_out[k, 1, rows] = im.T
            coh_out[k, rows] = coherent.T


def finish(at_head, parts, depth):
    chunks = len(parts)
    flat = [a for part in parts for a in part]
    blocks, lanes = flat[1].shape
    shapes = [(depth, 2, chunks * lanes, blocks)] * 2 + [(depth, chunks * lanes, blocks)]
    return pl.pallas_call(
        partial(finish_kernel, chunks),
        grid_spec=pltpu.PrefetchScalarGridSpec(
            num_scalar_prefetch=1,
            grid=(1,),
            in_specs=[small_spec(a.shape) for a in flat],
            out_specs=[small_spec(shape) for shape in shapes],
        ),
        out_shape=[jax.ShapeDtypeStruct(shape, F32) for shape in shapes],
        name="finish",
    )(at_head, *flat)


def swapped(block, axis, bit):
    return lax.ppermute(block, axis, [(i, i ^ (1 << bit)) for i in range(lax.axis_size(axis))])


def shifted(block, axis, distance):
    count = lax.axis_size(axis)
    return lax.ppermute(block, axis, [(i, i + distance) for i in range(count) if 0 <= i + distance < count])


def local(
    secondary,
    reference_store,
    tile_owner,
    az_kernel,
    rg_kernel,
    az_offset,
    az_index,
    rg_offset,
    rg_index,
):
    depth = secondary.shape[0]
    steps = reference_store.shape[1]
    count = LOOK_AZ // 2
    starts = range(0, steps, count)
    me = lax.axis_index("scene")
    bits = lax.axis_size("scene").bit_length() - 1
    core = (me & 1).astype(jnp.int32)[None]
    at_head = (me == 0).astype(jnp.int32)[None]

    def kept(bit, first, mine, other):
        same = ((tile_owner[first : first + count] ^ me) >> bit) & 1 == 0
        return jnp.where(same[:, None, None], mine, other)

    own, other = split_halves(reference_store, core)
    arrived = swapped(other, "scene", 0)
    z, head, tail, rg = azimuth(
        secondary, az_kernel, rg_kernel, az_offset, az_index, rg_offset, rg_index
    )
    held = [kept(0, f, own[f : f + count], arrived[f : f + count]) for f in starts]
    for bit in range(1, bits):
        held = [kept(bit, f, h, swapped(h, "scene", bit)) for f, h in zip(starts, held)]
    mates = [swapped(h, "scene", 0) for h in held]

    left = shifted(tail, "range", 1)
    right = shifted(head, "range", -1)
    parts = []
    for f, tile, mate in zip(starts, held, mates):
        *currents, seq, powers = range_resample(z, left, right, rg, f, count)
        handed = shifted(currents[-1], "scene", 1)
        pairs, pair_pow = reference_products(core, tile, mate, currents)
        lead, lead_pow = leading_products(handed, currents[0])
        parts.append((pairs, pair_pow, lead, lead_pow, seq, powers))
    return finish(at_head, parts, depth)


def solution(mesh):
    in_specs = (
        P(("parts", "scene"), None, None, "range"),
        P(("parts", "scene"), None, None, None, "range"),
        P("parts"),
        P(),
        P(),
        P(("parts", "scene"), None),
        P(("parts", "scene"), None),
        P(("parts", "scene"), "range"),
        P(("parts", "scene"), "range"),
    )
    out_specs = (
        P(("parts", "scene"), None, None, "range"),
        P(("parts", "scene"), None, None, "range"),
        P(("parts", "scene"), None, "range"),
    )
    return jax.shard_map(local, mesh=mesh, in_specs=in_specs, out_specs=out_specs, check_vma=False)
```

```python
from functools import partial

import jax
import jax.numpy as jnp
from jax import lax
from jax.experimental import pallas as pl
from jax.experimental.pallas import tpu as pltpu
from jax.sharding import PartitionSpec as P

TILE = 256
LOOK_AZ = 4
LOOK_RG = 16

eps_power = 1e-06

BF = jnp.bfloat16
F32 = jnp.float32
ACROSS = (((1,), (0,)), ((), ()))
OVER_ROWS = (((0,), (0,)), ((), ()))
OVER_LANES = (((1,), (1,)), ((), ()))
VMEM = pl.BlockSpec(memory_space=pltpu.VMEM)
SMALL = pltpu.CompilerParams(vmem_limit_bytes=12 << 20)


def iota(shape, dim):
    return lax.broadcasted_iota(jnp.int32, shape, dim)


def over(value, size):
    return value >> (size.bit_length() - 1)


def dot(a, b, dims=ACROSS):
    return lax.dot_general(a, b, dims, preferred_element_type=F32)


def lane_row(lane, half_rows):
    blocks = half_rows // LOOK_AZ
    inner = lane & (half_rows - 1)
    return LOOK_AZ * (inner & (blocks - 1)) + over(inner, blocks), over(lane, half_rows) & 1


def look_column(place, columns):
    blocks = columns // LOOK_RG
    return LOOK_RG * (place & (blocks - 1)) + over(place, blocks)


def chosen(shape, dim, wanted):
    return (iota(shape, dim) == wanted).astype(F32).astype(BF)


def taps_and_offsets(kernel_t, index_row, offset_row, spread):
    count = kernel_t.shape[1]
    taps = dot(kernel_t.astype(BF), chosen((count, index_row.shape[1]), 0, index_row))
    offsets = jnp.broadcast_to(offset_row.astype(F32), (8, offset_row.shape[1]))
    return dot(jnp.concatenate([taps, offsets], 0).astype(BF), spread)


def row_of(ref, k, columns):
    row = ref[0:1, columns]
    for other in range(1, ref.shape[0]):
        row = jnp.where(k == other, ref[other : other + 1, columns], row)
    return row


def split_kernel(half_ref, in_ref, out_ref, order_ref, columns_ref):
    half_rows, columns = in_ref.shape[2], in_ref.shape[4]
    s = pl.program_id(0)

    @pl.when(s == 0)
    def _():
        size = 2 * half_rows
        row, part = lane_row(iota((1, size), 1), half_rows)
        order_ref[...] = chosen((size, size), 0, 2 * row + part)
        columns_ref[...] = chosen((columns, columns), 1, look_column(iota((columns, 1), 0), columns))

    rows = in_ref[0, 0].reshape(2 * half_rows, columns)
    turned = dot(columns_ref[...], rows, OVER_LANES).astype(BF)
    out_ref[s] = dot(turned, order_ref[...]).astype(BF)


def split_half(reference_store, which):
    _, steps, tile, parts, columns = reference_store.shape
    half = tile // 2
    return pl.pallas_call(
        split_kernel,
        grid_spec=pltpu.PrefetchScalarGridSpec(
            num_scalar_prefetch=1,
            grid=(steps,),
            in_specs=[pl.BlockSpec((1, 1, half, parts, columns), lambda s, which: (0, s, which[0], 0, 0))],
            out_specs=VMEM,
            scratch_shapes=[
                pltpu.VMEM((parts * half, parts * half), BF),
                pltpu.VMEM((columns, columns), BF),
            ],
        ),
        out_shape=jax.ShapeDtypeStruct((steps, columns, parts * half), BF),
        compiler_params=SMALL,
        name="split_half",
    )(which, reference_store)


def azimuth_kernel(
    margin, x_ref, azk_ref, rgk_ref, azo_ref, azi_ref, rgo_ref, rgi_ref,
    z_ref, head_ref, tail_ref, rg_ref, spread_ref, band_ref,
):
    k, s = pl.program_id(0), pl.program_id(1)
    columns = x_ref.shape[3]
    taps = azk_ref.shape[0]
    lanes = spread_ref.shape[1]
    tile = lanes // 2
    half = tile // 2
    period = 2 * taps
    lane = iota((1, lanes), 1)
    row, part = lane_row(lane, half)
    row = row + half * over(lane, tile)

    @pl.when((k == 0) & (s == 0))
    def _():
        spread_ref[...] = chosen((tile, lanes), 0, row)

    @pl.when(s == 0)
    def _():
        column = look_column(iota((1, columns), 1), columns)
        everything = slice(0, columns)
        both = taps_and_offsets(
            rgk_ref[...],
            row_of(rgi_ref, k, everything),
            row_of(rgo_ref, k, everything),
            chosen((columns, columns), 0, column),
        )
        base = column + both[taps : taps + 1].astype(jnp.int32) + (margin - 3)
        sub = iota((period, columns), 0)
        place = sub - base
        which = place & (taps - 1)
        value = jnp.zeros((period, columns), F32)
        for tap in range(taps):
            value = jnp.where(which == tap, both[tap : tap + 1], value)
        for block in range(rg_ref.shape[1] // period):
            home = over(place + block * period, taps)
            rg_ref[k, block * period : (block + 1) * period] = jnp.where(home == 0, value, 0.0).astype(BF)

    start = pl.multiple_of(s * tile, tile)
    both = taps_and_offsets(
        azk_ref[...],
        row_of(azi_ref, k, pl.ds(start, tile)),
        row_of(azo_ref, k, pl.ds(start, tile)),
        spread_ref[...],
    )
    base = row + both[taps : taps + 1].astype(jnp.int32) + (margin - 3)
    sub = iota((period, lanes), 0)
    place = (sub >> 1) - base
    which = jnp.where((sub & 1) == part, place & (taps - 1), taps)
    value = jnp.zeros((period, lanes), F32)
    for tap in range(taps):
        value = jnp.where(which == tap, both[tap : tap + 1], value)
    home = -over(place, taps)
    for block in range(band_ref.shape[0] // period):
        band_ref[block * period : (block + 1) * period] = jnp.where(home == block, value, 0.0).astype(BF)
    rows = x_ref[0, pl.ds(start, tile + 2 * margin)].reshape(band_ref.shape[0], columns)
    z = dot(rows, band_ref[...], OVER_ROWS).astype(BF)
    z_ref[k, s] = z
    head_ref[k, s] = z[:margin]
    tail_ref[k, s] = z[columns - margin :]


def azimuth(secondary, az_kernel, rg_kernel, az_offset, az_index, rg_offset, rg_index):
    depth, rows, parts, columns = secondary.shape
    margin = (rows - az_offset.shape[1]) // 2
    steps = az_offset.shape[1] // TILE
    lanes = parts * TILE
    small = (az_kernel.T, rg_kernel.T, az_offset, az_index, rg_offset, rg_index)
    shapes = [
        (depth, steps, columns, lanes),
        (depth, steps, margin, lanes),
        (depth, steps, margin, lanes),
        (depth, columns + 2 * margin, columns),
    ]
    return pl.pallas_call(
        partial(azimuth_kernel, margin),
        grid=(depth, steps),
        in_specs=[pl.BlockSpec((1, rows, parts, columns), lambda k, s: (k, 0, 0, 0))] + [VMEM] * len(small),
        out_specs=[VMEM] * len(shapes),
        out_shape=[jax.ShapeDtypeStruct(shape, BF) for shape in shapes],
        scratch_shapes=[
            pltpu.VMEM((TILE, lanes), BF),
            pltpu.VMEM((parts * (TILE + 2 * margin), lanes), BF),
        ],
        compiler_params=SMALL,
        name="azimuth",
    )(secondary, *small)


def halves(block):
    width = block.shape[1] // 2
    wide = block.astype(F32)
    return wide[:, :width], wide[:, width:]


def looks(value):
    blocks = value.shape[0] // LOOK_RG
    total = value[:blocks]
    for look in range(1, LOOK_RG):
        total = total + value[look * blocks : (look + 1) * blocks]
    shift = value.shape[1] // 2
    while shift >= value.shape[1] // LOOK_AZ:
        total = total + pltpu.roll(total, shift, 1)
        shift //= 2
    return total * (1.0 / (LOOK_AZ * LOOK_RG))


def pair(first, second):
    a_re, a_im = first
    b_re, b_im = second
    return looks(a_re * b_re + a_im * b_im), looks(a_im * b_re - a_re * b_im)


def power(first):
    re, im = first
    return looks(re * re + im * im)


def joined(pieces):
    blocks = pieces[0].shape[1] // LOOK_AZ
    group = over(iota(pieces[0].shape, 1), blocks)
    total = pieces[0]
    for position in range(1, len(pieces)):
        total = jnp.where(group >= position, pieces[position], total)
    return total


def pairs_of(leads, followers):
    found = [pair(a, b) for a, b in zip(leads, followers)]
    return joined([re for re, _ in found]), joined([im for _, im in found])


def range_kernel(first, z_ref, head_ref, tail_ref, rg_ref, *outs):
    depth = z_ref.shape[0]
    cur_refs, (seq_ref, pow_ref) = outs[:depth], outs[depth:]
    before = None
    for k in range(depth):
        now = []
        for s in range(cur_refs[k].shape[0]):
            wide = jnp.concatenate([head_ref[k, first + s], z_ref[k, first + s], tail_ref[k, first + s]], 0)
            out = dot(rg_ref[k], wide, OVER_ROWS).astype(BF)
            width = out.shape[1] // 2
            for half in range(2):
                part = out[:, half * width : (half + 1) * width]
                cur_refs[k][s, half] = part
                now.append(part)
        pow_ref[k] = joined([power(halves(a)) for a in now])
        if k:
            seq_ref[k - 1, 0], seq_ref[k - 1, 1] = pairs_of(map(halves, before), map(halves, now))
        before = now


def range_resample(z, head, tail, rg, first, count):
    depth, _, columns, lanes = z.shape
    blocks, width = columns // LOOK_RG, lanes // 4
    current = jax.ShapeDtypeStruct((count, 2, columns, lanes // 2), BF)
    small = [(max(depth - 1, 1), 2, blocks, width), (depth, blocks, width)]
    return pl.pallas_call(
        partial(range_kernel, first),
        in_specs=[VMEM] * 4,
        out_specs=[VMEM] * (depth + 2),
        out_shape=[current] * depth + [jax.ShapeDtypeStruct(shape, F32) for shape in small],
        compiler_params=SMALL,
        name="range_resample",
    )(z, head, tail, rg)


def unit_refs(ref):
    return [ref.at[s, half] for s in range(ref.shape[0]) for half in range(2)]


def reference_kernel(core_ref, own_ref, mate_ref, *refs):
    depth = len(refs) - 2
    cur_refs, (pair_ref, pow_ref) = refs[:depth], refs[depth:]
    leads = []
    for s in range(own_ref.shape[0]):
        for half in range(2):
            leads.append(halves(jnp.where(core_ref[0] == half, own_ref[s], mate_ref[s])))
    pow_ref[...] = joined([power(a) for a in leads])
    for k in range(depth):
        pair_ref[k, 0], pair_ref[k, 1] = pairs_of(leads, [halves(r[...]) for r in unit_refs(cur_refs[k])])


def reference_products(core, own, mate, currents):
    _, columns, width = own.shape
    depth = len(currents)
    shapes = [(depth, 2, columns // LOOK_RG, width // 2), (columns // LOOK_RG, width // 2)]
    return pl.pallas_call(
        reference_kernel,
        in_specs=[pl.BlockSpec(memory_space=pltpu.SMEM)] + [VMEM] * (2 + depth),
        out_specs=[VMEM] * len(shapes),
        out_shape=[jax.ShapeDtypeStruct(shape, F32) for shape in shapes],
        compiler_params=SMALL,
        name="reference_products",
    )(core, own, mate, *currents)


def leading_kernel(lead_ref, cur_ref, out_ref):
    leads = [halves(r[...]) for r in unit_refs(lead_ref)]
    out_ref[0], out_ref[1] = pairs_of(leads, [halves(r[...]) for r in unit_refs(cur_ref)])
    out_ref[2] = joined([power(a) for a in leads])


def leading_products(lead, current):
    _, _, columns, width = lead.shape
    return pl.pallas_call(
        leading_kernel,
        in_specs=[VMEM] * 2,
        out_specs=VMEM,
        out_shape=jax.ShapeDtypeStruct((3, columns // LOOK_RG, width // 2), F32),
        compiler_params=SMALL,
        name="leading_products",
    )(lead, current)


def finish_kernel(head_ref, *refs):
    inputs, (ref_out, seq_out, coh_out) = refs[:-3], refs[-3:]
    at_head = head_ref[0] == 1
    lanes = inputs[1].shape[-1]
    for chunk in range(len(inputs) // 5):
        pairs, pair_pow, lead, seq, powers = inputs[5 * chunk : 5 * chunk + 5]
        rows = slice(chunk * lanes, (chunk + 1) * lanes)
        earlier = jnp.where(at_head, pair_pow[...], lead[2])
        for k in range(ref_out.shape[0]):
            if k:
                re, im = seq[k - 1, 0], seq[k - 1, 1]
            else:
                re = jnp.where(at_head, pairs[0, 0], lead[0])
                im = jnp.where(at_head, pairs[0, 1], lead[1])
            now = powers[k]
            ref_out[k, 0, :, rows] = pairs[k, 0]
            ref_out[k, 1, :, rows] = pairs[k, 1]
            seq_out[k, 0, :, rows] = re
            seq_out[k, 1, :, rows] = im
            coh_out[k, :, rows] = jnp.sqrt(re * re + im * im) / jnp.sqrt(earlier * now + eps_power)
            earlier = now


def finish(at_head, parts, depth):
    flat = [a for part in parts for a in part]
    blocks, lanes = flat[1].shape
    rows = len(parts) * lanes
    shapes = [(depth, 2, blocks, rows)] * 2 + [(depth, blocks, rows)]
    outs = pl.pallas_call(
        finish_kernel,
        in_specs=[pl.BlockSpec(memory_space=pltpu.SMEM)] + [VMEM] * len(flat),
        out_specs=[VMEM] * 3,
        out_shape=[jax.ShapeDtypeStruct(shape, F32) for shape in shapes],
        compiler_params=SMALL,
        name="finish",
    )(at_head, *flat)
    return tuple(jnp.swapaxes(a, -1, -2) for a in outs)


def swapped(block, axis, bit):
    return lax.ppermute(block, axis, [(i, i ^ (1 << bit)) for i in range(lax.axis_size(axis))])


def shifted(block, axis, distance):
    count = lax.axis_size(axis)
    return lax.ppermute(block, axis, [(i, i + distance) for i in range(count) if 0 <= i + distance < count])


def local(
    secondary,
    reference_store,
    tile_owner,
    az_kernel,
    rg_kernel,
    az_offset,
    az_index,
    rg_offset,
    rg_index,
):
    depth = secondary.shape[0]
    steps = reference_store.shape[1]
    count = LOOK_AZ // 2
    starts = range(0, steps, count)
    me = lax.axis_index("scene")
    bits = lax.axis_size("scene").bit_length() - 1
    core = (me & 1).astype(jnp.int32)[None]
    at_head = (me == 0).astype(jnp.int32)[None]

    def kept(bit, first, mine, other):
        same = ((tile_owner[first : first + count] ^ me) >> bit) & 1 == 0
        return jnp.where(same[:, None, None], mine, other)

    other = split_half(reference_store, 1 - core)
    arrived = swapped(other, "scene", 0)
    own = split_half(reference_store, core)
    held = [kept(0, f, own[f : f + count], arrived[f : f + count]) for f in starts]
    for bit in range(1, bits):
        held = [kept(bit, f, h, swapped(h, "scene", bit)) for f, h in zip(starts, held)]
    z, head, tail, rg = azimuth(
        secondary, az_kernel, rg_kernel, az_offset, az_index, rg_offset, rg_index
    )
    mates = [swapped(h, "scene", 0) for h in held]

    left = shifted(tail, "range", 1)
    right = shifted(head, "range", -1)
    parts = []
    for n, (f, tile, mate) in enumerate(zip(starts, held, mates)):
        *currents, seq, powers = range_resample(z, left, right, rg, f, count)
        if n % 2:
            handed = shifted(currents[0], "scene", -1)
            lead = shifted(leading_products(currents[-1], handed), "scene", 1)
        else:
            handed = shifted(currents[-1], "scene", 1)
            lead = leading_products(handed, currents[0])
        pairs, pair_pow = reference_products(core, tile, mate, currents)
        parts.append((pairs, pair_pow, lead, seq, powers))
    return finish(at_head, parts, depth)


def solution(mesh):
    in_specs = (
        P(("parts", "scene"), None, None, "range"),
        P(("parts", "scene"), None, None, None, "range"),
        P("parts"),
        P(),
        P(),
        P(("parts", "scene"), None),
        P(("parts", "scene"), None),
        P(("parts", "scene"), "range"),
        P(("parts", "scene"), "range"),
    )
    out_specs = (
        P(("parts", "scene"), None, None, "range"),
        P(("parts", "scene"), None, None, "range"),
        P(("parts", "scene"), None, "range"),
    )
    return jax.shard_map(local, mesh=mesh, in_specs=in_specs, out_specs=out_specs, check_vma=False)
```

```python
from functools import partial

import jax
import jax.numpy as jnp
from jax import lax
from jax.experimental import pallas as pl
from jax.experimental.pallas import tpu as pltpu
from jax.sharding import PartitionSpec as P


TILE = 256
LOOK_AZ = 4
LOOK_RG = 16

eps_power = 1e-06

BF = jnp.bfloat16
F32 = jnp.float32
ACROSS = (((1,), (0,)), ((), ()))
OVER_ROWS = (((0,), (0,)), ((), ()))
OVER_LANES = (((1,), (1,)), ((), ()))
VMEM = pl.BlockSpec(memory_space=pltpu.VMEM)
SMEM = pl.BlockSpec(memory_space=pltpu.SMEM)
SMALL = pltpu.CompilerParams(vmem_limit_bytes=12 << 20)


def iota(shape, dim):
    return lax.broadcasted_iota(jnp.int32, shape, dim)


def over(value, size):
    return value >> (size.bit_length() - 1)


def dot(a, b, dims=ACROSS):
    return lax.dot_general(a, b, dims, preferred_element_type=F32)


def lane_row(lane, half_rows):
    blocks = half_rows // LOOK_AZ
    inner = lane & (half_rows - 1)
    return LOOK_AZ * (inner & (blocks - 1)) + over(inner, blocks), over(lane, half_rows) & 1


def look_column(place, columns):
    blocks = columns // LOOK_RG
    return LOOK_RG * (place & (blocks - 1)) + over(place, blocks)


def chosen(shape, dim, wanted):
    return (iota(shape, dim) == wanted).astype(F32).astype(BF)


def taps_and_offsets(kernel_t, index_row, offset_row, spread):
    count = kernel_t.shape[1]
    taps = dot(kernel_t.astype(BF), chosen((count, index_row.shape[1]), 0, index_row))
    offsets = jnp.broadcast_to(offset_row.astype(F32), (8, offset_row.shape[1]))
    return dot(jnp.concatenate([taps, offsets], 0).astype(BF), spread)


def resident(*arrays):
    return [pltpu.with_memory_space_constraint(a, pltpu.VMEM) for a in arrays]


def load_kernel(margin, x_ref, *refs):
    count = (len(refs) - 4) // 2
    small_refs, x_out, outs = refs[:count], refs[count], refs[count + 1 : 2 * count + 1]
    head_ref, tail_ref, sems = refs[2 * count + 1 :]
    depth, rows, parts, columns = x_ref.shape
    pieces = [(k, n) for k in range(depth) for n in range(rows // TILE)]

    def copy_of(position):
        k, n = pieces[position]
        size = TILE if n + 1 < rows // TILE else rows - n * TILE
        part = (k, pl.ds(n * TILE, size))
        return pltpu.make_async_copy(x_ref.at[part], x_out.at[part], sems.at[position]), part, size

    copies = [copy_of(position) for position in range(len(pieces))]
    small = [
        pltpu.make_async_copy(source, target, sems.at[len(pieces) + n])
        for n, (source, target) in enumerate(zip(small_refs, outs))
    ]
    for copy, _, _ in copies:
        copy.start()
    for copy in small:
        copy.start()
    place = iota((2 * margin, 1), 0)
    edges = chosen((2 * margin, columns), 1, jnp.where(place < margin, place, place + columns - 2 * margin))
    for (k, n), (copy, part, size) in zip(pieces, copies):
        copy.wait()
        found = dot(edges, x_out[part].reshape(parts * size, columns), OVER_LANES).astype(BF)
        lanes = slice(parts * n * TILE, parts * (n * TILE + size))
        head_ref[k, :, lanes] = found[:margin]
        tail_ref[k, :, lanes] = found[margin:]
    for copy in small:
        copy.wait()


def load(secondary, *small):
    depth, rows, parts, _ = secondary.shape
    margin = (rows - small[-1].shape[1]) // 2
    operands = (secondary, *small)
    edge = pltpu.VMEM((depth, margin, parts * rows), BF)
    anywhere = pl.BlockSpec(memory_space=pl.ANY)
    outs = pl.pallas_call(
        partial(load_kernel, margin),
        in_specs=[anywhere] * len(operands),
        out_specs=[VMEM] * (len(operands) + 2),
        out_shape=[pltpu.VMEM(a.shape, a.dtype) for a in operands] + [edge, edge],
        scratch_shapes=[pltpu.SemaphoreType.DMA((depth * (rows // TILE) + len(small),))],
        compiler_params=SMALL,
        name="load",
    )(*[pltpu.with_memory_space_constraint(a, pltpu.HBM) for a in operands])
    return outs[:-2], outs[-2], outs[-1]


def range_matrix(margin, kernel_ref, index_row, offset_row, order, column, rg_ref):
    taps = kernel_ref.shape[0]
    both = taps_and_offsets(kernel_ref[...], index_row, offset_row, order)
    base = column + both[taps : taps + 1].astype(jnp.int32) + (margin - 3)
    period = 2 * taps
    place = iota((period, order.shape[1]), 0) - base
    value = tap_pattern(both, place & (taps - 1))
    for block in range(rg_ref.shape[0] // period):
        home = over(place + block * period, taps)
        rg_ref[block * period : (block + 1) * period] = jnp.where(home == 0, value, 0.0).astype(BF)


def tap_pattern(both, which):
    value = jnp.zeros(which.shape, F32)
    for tap in range(both.shape[0] - 8):
        value = jnp.where(which == tap, both[tap : tap + 1], value)
    return value


def resample_kernel(
    margin, x_ref, azk_ref, rgk_ref, rgo_ref, rgi_ref, azi_ref, azo_ref, left_ref, right_ref,
    *refs,
):
    depth, _, _, columns = x_ref.shape
    outs, (spread_ref, band_ref, rg_ref) = refs[:-3], refs[-3:]
    taps = azk_ref.shape[0]
    tile, lanes = spread_ref.shape
    half_rows, half_lanes = tile // 2, lanes // 2
    period = 2 * taps
    lane = iota((1, lanes), 1)
    row, part = lane_row(lane, half_rows)
    spread_ref[...] = chosen((tile, lanes), 0, row + half_rows * over(lane, half_lanes))
    column = look_column(iota((1, columns), 1), columns)
    order = chosen((columns, columns), 0, column)
    for k in range(depth):
        range_matrix(
            margin, rgk_ref, rgi_ref[k : k + 1], rgo_ref[k : k + 1], order, column, rg_ref.at[k]
        )
    for n in range(len(outs) // (depth + 2)):
        *cur_refs, seq_ref, pow_ref = outs[n * (depth + 2) : (n + 1) * (depth + 2)]
        before = None
        for k in range(depth):
            now = []
            for s in range(2):
                start = (2 * n + s) * tile
                rows = slice(start, start + tile)
                both = taps_and_offsets(
                    azk_ref[...], azi_ref[k : k + 1, rows], azo_ref[k : k + 1, rows], spread_ref[...]
                )
                base = row + both[taps : taps + 1].astype(jnp.int32) + (margin - 3)
                sub = iota((period, lanes), 0)
                place = (sub >> 1) - base
                value = tap_pattern(both, jnp.where((sub & 1) == part, place & (taps - 1), taps))
                home = -over(place, taps)
                for half in range(2):
                    mine = slice(half * half_lanes, (half + 1) * half_lanes)
                    band = band_ref.at[k % 2, s, half]
                    for block in range(band.shape[0] // period):
                        band[block * period : (block + 1) * period] = jnp.where(
                            home[:, mine] == block, value[:, mine], 0.0
                        ).astype(BF)
                    first = start + half * half_rows
                    size = half_rows + 2 * margin
                    window = x_ref[k, first : first + size].reshape(2 * size, columns)
                    across = slice(2 * first, 2 * (first + size))
                    wide = jnp.concatenate(
                        [
                            dot(left_ref[k, :, across], band[...]).astype(BF),
                            dot(window, band[...], OVER_ROWS).astype(BF),
                            dot(right_ref[k, :, across], band[...]).astype(BF),
                        ],
                        0,
                    )
                    out = dot(rg_ref[k], wide, OVER_ROWS).astype(BF)
                    cur_refs[k][s, half] = out
                    now.append(out)
            pow_ref[k] = joined([power(halves(a)) for a in now])
            if k:
                seq_ref[k - 1, 0], seq_ref[k - 1, 1] = pairs_of(map(halves, before), map(halves, now))
            before = now


def resample(operands, left, right):
    depth, rows, parts, columns = operands[0].shape
    margin = left.shape[1]
    chunks = (rows - 2 * margin) // TILE // 2
    lanes = parts * TILE
    blocks, width = columns // LOOK_RG, lanes // 4
    shapes = [pltpu.VMEM((2, 2, columns, lanes // 2), BF)] * depth
    shapes += [pltpu.VMEM((max(depth - 1, 1), 2, blocks, width), F32), pltpu.VMEM((depth, blocks, width), F32)]
    arrays = resident(*operands, left, right)
    outs = pl.pallas_call(
        partial(resample_kernel, margin),
        in_specs=[VMEM] * len(arrays),
        out_specs=[VMEM] * len(shapes) * chunks,
        out_shape=shapes * chunks,
        scratch_shapes=[
            pltpu.VMEM((TILE, lanes), BF),
            pltpu.VMEM((2, 2, 2, parts * (TILE // 2 + 2 * margin), lanes // 2), BF),
            pltpu.VMEM((depth, columns + 2 * margin, columns), BF),
        ],
        compiler_params=SMALL,
        name="resample",
    )(*arrays)
    return [outs[n * len(shapes) : (n + 1) * len(shapes)] for n in range(chunks)]


def choose_kernel(first, bit, stored, owner_ref, me_ref, *refs):
    sources, outs, sems = refs[:2], refs[2:-1], refs[-1]
    me = me_ref[0]
    copies = []
    for n, out in enumerate(outs):
        tile = 2 * (first + n) + (me & 1)
        here, there = [ref.at[0, tile] if stored else ref for ref in sources]
        same = ((owner_ref[tile] ^ me) >> bit) & 1 == 0
        copies.append(pltpu.make_async_copy(here, out, sems.at[n]))
        pl.when(same)(copies[n].start)
        pl.when(jnp.logical_not(same))(pltpu.make_async_copy(there, out, sems.at[n]).start)
    for copy in copies:
        copy.wait()


def choose(owner, me, here, there, first, bit, chunks):
    anywhere = pl.BlockSpec(memory_space=pl.ANY)
    return pl.pallas_call(
        partial(choose_kernel, first, bit, here.ndim > 3),
        in_specs=[SMEM, SMEM, anywhere, anywhere],
        out_specs=[VMEM] * chunks,
        out_shape=[pltpu.VMEM(here.shape[-3:], BF)] * chunks,
        scratch_shapes=[pltpu.SemaphoreType.DMA((chunks,))],
        compiler_params=SMALL,
        name="choose",
    )(owner, me, here, there)


def halves(block):
    width = block.shape[1] // 2
    wide = block.astype(F32)
    return wide[:, :width], wide[:, width:]


def looks(value):
    blocks = value.shape[0] // LOOK_RG
    total = value[:blocks]
    for look in range(1, LOOK_RG):
        total = total + value[look * blocks : (look + 1) * blocks]
    shift = value.shape[1] // 2
    while shift >= value.shape[1] // LOOK_AZ:
        total = total + pltpu.roll(total, shift, 1)
        shift //= 2
    return total * (1.0 / (LOOK_AZ * LOOK_RG))


def pair(first, second):
    a_re, a_im = first
    b_re, b_im = second
    return looks(a_re * b_re + a_im * b_im), looks(a_im * b_re - a_re * b_im)


def power(first):
    re, im = first
    return looks(re * re + im * im)


def joined(pieces):
    blocks = pieces[0].shape[1] // LOOK_AZ
    group = over(iota(pieces[0].shape, 1), blocks)
    total = pieces[0]
    for position in range(1, len(pieces)):
        total = jnp.where(group >= position, pieces[position], total)
    return total


def pairs_of(leads, followers):
    found = [pair(a, b) for a, b in zip(leads, followers)]
    return joined([re for re, _ in found]), joined([im for _, im in found])


def unit_refs(ref):
    return [ref.at[s, half] for s in range(ref.shape[0]) for half in range(2)]


def reference_kernel(me_ref, own_ref, mate_ref, *refs):
    depth = len(refs) - 2
    cur_refs, (pair_ref, pow_ref) = refs[:depth], refs[depth:]
    columns, half_rows = own_ref.shape[2], own_ref.shape[0] // 2
    core = me_ref[0] & 1
    size = 2 * half_rows
    row, part = lane_row(iota((1, size), 1), half_rows)
    order = chosen((size, size), 0, 2 * row + part)
    turn = chosen((columns, columns), 1, look_column(iota((columns, 1), 0), columns))
    powers, pairs = [], [[] for _ in range(depth)]
    for ref, place in ((own_ref, core), (mate_ref, 1 - core)):
        for half in range(2):
            rows = ref[half * half_rows : (half + 1) * half_rows].reshape(size, columns)
            lead = dot(turn, dot(rows, order, OVER_ROWS).astype(BF))
            lead = lead[:, :half_rows], lead[:, half_rows:]
            powers.append(power(lead))
            for k in range(depth):
                pairs[k].append(pair(lead, halves(cur_refs[k][place, half])))

    def in_order(pieces):
        return joined([jnp.where(core == 0, pieces[n], pieces[(n + 2) % 4]) for n in range(4)])

    pow_ref[...] = in_order(powers)
    for k in range(depth):
        pair_ref[k, 0] = in_order([re for re, _ in pairs[k]])
        pair_ref[k, 1] = in_order([im for _, im in pairs[k]])


def reference_products(me, own, mate, currents):
    _, _, columns, width = currents[0].shape
    depth = len(currents)
    shapes = [(depth, 2, columns // LOOK_RG, width // 2), (columns // LOOK_RG, width // 2)]
    return pl.pallas_call(
        reference_kernel,
        in_specs=[SMEM] + [VMEM] * (2 + depth),
        out_specs=[VMEM] * len(shapes),
        out_shape=[pltpu.VMEM(shape, F32) for shape in shapes],
        compiler_params=SMALL,
        name="reference_products",
    )(me, *resident(own, mate, *currents))


def leading_kernel(lead_ref, cur_ref, out_ref):
    leads = [halves(r[...]) for r in unit_refs(lead_ref)]
    out_ref[0], out_ref[1] = pairs_of(leads, [halves(r[...]) for r in unit_refs(cur_ref)])
    out_ref[2] = joined([power(a) for a in leads])


def leading_products(lead, current):
    _, _, columns, width = lead.shape
    return pl.pallas_call(
        leading_kernel,
        in_specs=[VMEM] * 2,
        out_specs=VMEM,
        out_shape=pltpu.VMEM((3, columns // LOOK_RG, width // 2), F32),
        compiler_params=SMALL,
        name="leading_products",
    )(*resident(lead, current))


def finish_kernel(me_ref, *refs):
    inputs, (ref_out, seq_out, coh_out) = refs[:-3], refs[-3:]
    at_head = me_ref[0] == 0
    lanes = inputs[1].shape[-1]
    for chunk in range(len(inputs) // 5):
        pairs, pair_pow, lead, seq, powers = inputs[5 * chunk : 5 * chunk + 5]
        rows = slice(chunk * lanes, (chunk + 1) * lanes)
        earlier = jnp.where(at_head, pair_pow[...], lead[2])
        for k in range(ref_out.shape[0]):
            if k:
                re, im = seq[k - 1, 0], seq[k - 1, 1]
            else:
                re = jnp.where(at_head, pairs[0, 0], lead[0])
                im = jnp.where(at_head, pairs[0, 1], lead[1])
            now = powers[k]
            ref_out[k, 0, :, rows] = pairs[k, 0]
            ref_out[k, 1, :, rows] = pairs[k, 1]
            seq_out[k, 0, :, rows] = re
            seq_out[k, 1, :, rows] = im
            coh_out[k, :, rows] = jnp.sqrt(re * re + im * im) / jnp.sqrt(earlier * now + eps_power)
            earlier = now


def finish(me, parts, depth):
    flat = [a for part in parts for a in part]
    blocks, lanes = flat[1].shape
    rows = len(parts) * lanes
    shapes = [(depth, 2, blocks, rows)] * 2 + [(depth, blocks, rows)]
    outs = pl.pallas_call(
        finish_kernel,
        in_specs=[SMEM] + [VMEM] * len(flat),
        out_specs=[VMEM] * 3,
        out_shape=[jax.ShapeDtypeStruct(shape, F32) for shape in shapes],
        compiler_params=SMALL,
        name="finish",
    )(me, *resident(*flat))
    return tuple(jnp.swapaxes(a, -1, -2) for a in outs)


def swapped(block, axis, bit):
    return lax.ppermute(block, axis, [(i, i ^ (1 << bit)) for i in range(lax.axis_size(axis))])


def shifted(block, axis, distance):
    count = lax.axis_size(axis)
    return lax.ppermute(block, axis, [(i, i + distance) for i in range(count) if 0 <= i + distance < count])


def local(
    secondary,
    reference_store,
    tile_owner,
    az_kernel,
    rg_kernel,
    az_offset,
    az_index,
    rg_offset,
    rg_index,
):
    depth = secondary.shape[0]
    chunks = reference_store.shape[1] // 2
    bits = lax.axis_size("scene").bit_length() - 1
    me = lax.axis_index("scene").astype(jnp.int32)[None]

    arrived = swapped(reference_store, "scene", 0)
    operands, head, tail = load(
        secondary, az_kernel.T, rg_kernel.T, rg_offset, rg_index, az_index, az_offset
    )
    stored, owner = (pltpu.with_memory_space_constraint(a, pltpu.HBM) for a in (reference_store, tile_owner))
    held = list(choose(owner, me, stored, arrived, 0, 0, chunks))
    for bit in range(1, bits):
        for n in range(chunks):
            got = swapped(held[n], "scene", bit)
            held[n] = choose(owner, me, held[n], got, n, bit, 1)[0]
    left = shifted(tail, "range", 1)
    right = shifted(head, "range", -1)
    resampled = resample(operands, left, right)
    results = []
    for n, (*currents, seq, powers) in enumerate(resampled):
        backward = n % 2
        handed = shifted(currents[0], "scene", -1) if backward else shifted(currents[-1], "scene", 1)
        if backward:
            lead = leading_products(currents[-1], handed)
            lead = shifted(lead, "scene", 1)
        else:
            lead = leading_products(handed, currents[0])
        mate = swapped(held[n], "scene", 0)
        pairs, pair_pow = reference_products(me, held[n], mate, currents)
        results.append((pairs, pair_pow, lead, seq, powers))
    return finish(me, results, depth)


def solution(mesh):
    in_specs = (
        P(("parts", "scene"), None, None, "range"),
        P(("parts", "scene"), None, None, None, "range"),
        P("parts"),
        P(),
        P(),
        P(("parts", "scene"), None),
        P(("parts", "scene"), None),
        P(("parts", "scene"), "range"),
        P(("parts", "scene"), "range"),
    )
    out_specs = (
        P(("parts", "scene"), None, None, "range"),
        P(("parts", "scene"), None, None, "range"),
        P(("parts", "scene"), None, "range"),
    )
    return jax.shard_map(local, mesh=mesh, in_specs=in_specs, out_specs=out_specs, check_vma=False)
```

```python
from functools import partial

import jax
import jax.numpy as jnp
from jax import lax
from jax.experimental import pallas as pl
from jax.experimental.pallas import tpu as pltpu
from jax.sharding import PartitionSpec as P


TILE = 256
PIECE = 64
LOOK_AZ = 4
LOOK_RG = 16

eps_power = 1e-06

BF = jnp.bfloat16
F32 = jnp.float32
ACROSS = (((1,), (0,)), ((), ()))
OVER_ROWS = (((0,), (0,)), ((), ()))
OVER_LANES = (((1,), (1,)), ((), ()))
VMEM = pl.BlockSpec(memory_space=pltpu.VMEM)
SMEM = pl.BlockSpec(memory_space=pltpu.SMEM)
SMALL = pltpu.CompilerParams(vmem_limit_bytes=12 << 20)


def iota(shape, dim):
    return lax.broadcasted_iota(jnp.int32, shape, dim)


def over(value, size):
    return value >> (size.bit_length() - 1)


def dot(a, b, dims=ACROSS):
    return lax.dot_general(a, b, dims, preferred_element_type=F32)


def lane_row(lane, half_rows):
    blocks = half_rows // LOOK_AZ
    inner = lane & (half_rows - 1)
    return LOOK_AZ * (inner & (blocks - 1)) + over(inner, blocks), over(lane, half_rows) & 1


def look_column(place, columns):
    blocks = columns // LOOK_RG
    return LOOK_RG * (place & (blocks - 1)) + over(place, blocks)


def chosen(shape, dim, wanted):
    return (iota(shape, dim) == wanted).astype(F32).astype(BF)


def taps_and_offsets(kernel_t, index_row, offset_row, spread):
    count = kernel_t.shape[1]
    taps = dot(kernel_t.astype(BF), chosen((count, index_row.shape[1]), 0, index_row))
    offsets = jnp.broadcast_to(offset_row.astype(F32), (8, offset_row.shape[1]))
    return dot(jnp.concatenate([taps, offsets], 0).astype(BF), spread)


def resident(*arrays):
    return [pltpu.with_memory_space_constraint(a, pltpu.VMEM) for a in arrays]


def load_kernel(margin, x_ref, *refs):
    count = (len(refs) - 4) // 2
    small_refs, x_out, outs = refs[:count], refs[count], refs[count + 1 : 2 * count + 1]
    first_ref, second_ref, sems = refs[2 * count + 1 :]
    depth, rows, parts, columns = x_ref.shape
    pieces = [(k, n) for k in range(depth) for n in range(rows // TILE)]

    def copy_of(position):
        k, n = pieces[position]
        size = TILE if n + 1 < rows // TILE else rows - n * TILE
        part = (k, pl.ds(n * TILE, size))
        return pltpu.make_async_copy(x_ref.at[part], x_out.at[part], sems.at[position]), part, size

    copies = [copy_of(position) for position in range(len(pieces))]
    small = [
        pltpu.make_async_copy(source, target, sems.at[len(pieces) + n])
        for n, (source, target) in enumerate(zip(small_refs, outs))
    ]
    for copy, _, _ in copies:
        copy.start()
    for copy in small:
        copy.start()
    place = iota((2 * margin, 1), 0)
    right_first = place + jnp.where(place < margin, columns - margin, -margin)
    left_first = place + jnp.where(place < margin, 0, columns - 2 * margin)
    edges = chosen((2 * margin, columns), 1, jnp.where(lax.axis_index("range") & 1 == 0, right_first, left_first))
    for (k, n), (copy, part, size) in zip(pieces, copies):
        copy.wait()
        found = dot(edges, x_out[part].reshape(parts * size, columns), OVER_LANES).astype(BF)
        lanes = slice(parts * n * TILE, parts * (n * TILE + size))
        first_ref[k, :, lanes] = found[:margin]
        second_ref[k, :, lanes] = found[margin:]
    for copy in small:
        copy.wait()


def load(secondary, *small):
    depth, rows, parts, _ = secondary.shape
    margin = (rows - small[-1].shape[1]) // 2
    operands = (secondary, *small)
    edge = pltpu.VMEM((depth, margin, parts * rows), BF)
    anywhere = pl.BlockSpec(memory_space=pl.ANY)
    outs = pl.pallas_call(
        partial(load_kernel, margin),
        in_specs=[anywhere] * len(operands),
        out_specs=[VMEM] * (len(operands) + 2),
        out_shape=[pltpu.VMEM(a.shape, a.dtype) for a in operands] + [edge, edge],
        scratch_shapes=[pltpu.SemaphoreType.DMA((depth * (rows // TILE) + len(small),))],
        compiler_params=SMALL,
        name="load",
    )(*[pltpu.with_memory_space_constraint(a, pltpu.HBM) for a in operands])
    return outs[:-2], outs[-2], outs[-1]


def range_matrix(margin, kernel_ref, index_row, offset_row, order, column, rg_ref):
    taps = kernel_ref.shape[0]
    both = taps_and_offsets(kernel_ref[...], index_row, offset_row, order)
    base = column + both[taps : taps + 1].astype(jnp.int32) + (margin - 3)
    period = 2 * taps
    place = iota((period, order.shape[1]), 0) - base
    value = tap_pattern(both, place & (taps - 1))
    for block in range(rg_ref.shape[0] // period):
        home = over(place + block * period, taps)
        rg_ref[block * period : (block + 1) * period] = jnp.where(home == 0, value, 0.0).astype(BF)


def tap_pattern(both, which):
    value = jnp.zeros(which.shape, F32)
    for tap in range(both.shape[0] - 8):
        value = jnp.where(which == tap, both[tap : tap + 1], value)
    return value


def resample_kernel(
    calls, x_ref, azk_ref, rgk_ref, rgo_ref, rgi_ref, azi_ref, azo_ref, first_ref, second_ref, *refs,
):
    columns = x_ref.shape[3]
    margin = first_ref.shape[1]
    outs, (spread_ref, band_ref, rg_ref) = refs[: len(calls)], refs[len(calls) :]
    odd_column = lax.axis_index("range") & 1 == 1
    taps = azk_ref.shape[0]
    tile, lanes = spread_ref.shape
    half_rows, half_lanes = tile // 2, lanes // 2
    period = 2 * taps
    lane = iota((1, lanes), 1)
    row, part = lane_row(lane, half_rows)
    spread_ref[...] = chosen((tile, lanes), 0, row + half_rows * over(lane, half_lanes))
    column = look_column(iota((1, columns), 1), columns)
    order = chosen((columns, columns), 0, column)
    for k in sorted({k for k, _ in calls}):
        range_matrix(
            margin, rgk_ref, rgi_ref[k : k + 1], rgo_ref[k : k + 1], order, column, rg_ref.at[k]
        )
    for call, (k, chunk) in enumerate(calls):
        for s in range(2):
            start = (2 * chunk + s) * tile
            rows = slice(start, start + tile)
            both = taps_and_offsets(
                azk_ref[...], azi_ref[k : k + 1, rows], azo_ref[k : k + 1, rows], spread_ref[...]
            )
            base = row + both[taps : taps + 1].astype(jnp.int32) + (margin - 3)
            sub = iota((period, lanes), 0)
            place = (sub >> 1) - base
            value = tap_pattern(both, jnp.where((sub & 1) == part, place & (taps - 1), taps))
            home = -over(place, taps)
            for half in range(2):
                mine = slice(half * half_lanes, (half + 1) * half_lanes)
                band = band_ref.at[call % 2, s, half]
                for block in range(band.shape[0] // period):
                    band[block * period : (block + 1) * period] = jnp.where(
                        home[:, mine] == block, value[:, mine], 0.0
                    ).astype(BF)
                begin = start + half * half_rows
                size = half_rows + 2 * margin
                window = x_ref[k, begin : begin + size].reshape(2 * size, columns)
                across = slice(2 * begin, 2 * (begin + size))
                first_side, second_side = first_ref[k, :, across], second_ref[k, :, across]
                wide = jnp.concatenate(
                    [
                        dot(jnp.where(odd_column, first_side, second_side), band[...]).astype(BF),
                        dot(window, band[...], OVER_ROWS).astype(BF),
                        dot(jnp.where(odd_column, second_side, first_side), band[...]).astype(BF),
                    ],
                    0,
                )
                outs[call][s, half] = dot(rg_ref[k], wide, OVER_ROWS).astype(BF)


def resample(operands, first, second, calls):
    depth, _, parts, columns = operands[0].shape
    margin = first.shape[1]
    lanes = parts * TILE
    arrays = resident(*operands, first, second)
    return pl.pallas_call(
        partial(resample_kernel, calls),
        in_specs=[VMEM] * len(arrays),
        out_specs=[VMEM] * len(calls),
        out_shape=[pltpu.VMEM((2, 2, columns, lanes // 2), BF)] * len(calls),
        scratch_shapes=[
            pltpu.VMEM((TILE, lanes), BF),
            pltpu.VMEM((2, 2, 2, parts * (TILE // 2 + 2 * margin), lanes // 2), BF),
            pltpu.VMEM((depth, columns + 2 * margin, columns), BF),
        ],
        compiler_params=SMALL,
        name="resample",
    )(*arrays)


def choose_kernel(first, bit, stored, owner_ref, *refs):
    sources, outs, sems = refs[:2], refs[2:-1], refs[-1]
    me = lax.axis_index("scene")
    copies = []
    for n, out in enumerate(outs):
        tile = 2 * (first + n) + (me & 1)
        here, there = [ref.at[0, tile] if stored else ref for ref in sources]
        same = ((owner_ref[tile] ^ me) >> bit) & 1 == 0
        pieces = [pl.ds(m * PIECE, PIECE) for m in range(out.shape[0] // PIECE)]
        from_here, from_there = [
            [pltpu.make_async_copy(source.at[p], out.at[p], sems.at[n, m]) for m, p in enumerate(pieces)]
            for source in (here, there)
        ]

        @pl.when(same)
        def _():
            for copy in from_here:
                copy.start()

        @pl.when(jnp.logical_not(same))
        def _():
            for copy in from_there:
                copy.start()

        copies += from_here
    for copy in copies:
        copy.wait()


def choose(owner, here, there, first, bit, chunks):
    anywhere = pl.BlockSpec(memory_space=pl.ANY)
    return pl.pallas_call(
        partial(choose_kernel, first, bit, here.ndim > 3),
        in_specs=[SMEM, anywhere, anywhere],
        out_specs=[VMEM] * chunks,
        out_shape=[pltpu.VMEM(here.shape[-3:], BF)] * chunks,
        scratch_shapes=[pltpu.SemaphoreType.DMA((chunks, here.shape[-3] // PIECE))],
        compiler_params=SMALL,
        name="choose",
    )(owner, here, there)


def halves(block):
    width = block.shape[1] // 2
    wide = block.astype(F32)
    return wide[:, :width], wide[:, width:]


def looks(value):
    blocks = value.shape[0] // LOOK_RG
    total = value[:blocks]
    for look in range(1, LOOK_RG):
        total = total + value[look * blocks : (look + 1) * blocks]
    shift = value.shape[1] // 2
    while shift >= value.shape[1] // LOOK_AZ:
        total = total + pltpu.roll(total, shift, 1)
        shift //= 2
    return total * (1.0 / (LOOK_AZ * LOOK_RG))


def pair(first, second):
    a_re, a_im = first
    b_re, b_im = second
    return looks(a_re * b_re + a_im * b_im), looks(a_im * b_re - a_re * b_im)


def power(first):
    re, im = first
    return looks(re * re + im * im)


def joined(pieces):
    blocks = pieces[0].shape[1] // LOOK_AZ
    group = over(iota(pieces[0].shape, 1), blocks)
    total = pieces[0]
    for position in range(1, len(pieces)):
        total = jnp.where(group >= position, pieces[position], total)
    return total


def pairs_of(leads, followers):
    found = [pair(a, b) for a, b in zip(leads, followers)]
    return joined([re for re, _ in found]), joined([im for _, im in found])


def reference_kernel(own_ref, mate_ref, *refs):
    depth = len(refs) - 2
    cur_refs, (pair_ref, pow_ref) = refs[:depth], refs[depth:]
    columns, half_rows = own_ref.shape[2], own_ref.shape[0] // 2
    core = lax.axis_index("scene") & 1
    size = 2 * half_rows
    row, part = lane_row(iota((1, size), 1), half_rows)
    order = chosen((size, size), 0, 2 * row + part)
    turn = chosen((columns, columns), 1, look_column(iota((columns, 1), 0), columns))
    powers, pairs = [], [[] for _ in range(depth)]
    for ref, place in ((own_ref, core), (mate_ref, 1 - core)):
        for half in range(2):
            rows = ref[half * half_rows : (half + 1) * half_rows].reshape(size, columns)
            lead = dot(turn, dot(rows, order, OVER_ROWS).astype(BF))
            lead = lead[:, :half_rows], lead[:, half_rows:]
            powers.append(power(lead))
            for k in range(depth):
                pairs[k].append(pair(lead, halves(cur_refs[k][place, half])))

    def in_order(pieces):
        return joined([jnp.where(core == 0, pieces[n], pieces[(n + 2) % 4]) for n in range(4)])

    pow_ref[...] = in_order(powers)
    for k in range(depth):
        pair_ref[k, 0] = in_order([re for re, _ in pairs[k]])
        pair_ref[k, 1] = in_order([im for _, im in pairs[k]])


def reference_products(own, mate, currents):
    _, _, columns, width = currents[0].shape
    depth = len(currents)
    shapes = [(depth, 2, columns // LOOK_RG, width // 2), (columns // LOOK_RG, width // 2)]
    return pl.pallas_call(
        reference_kernel,
        in_specs=[VMEM] * (2 + depth),
        out_specs=[VMEM] * len(shapes),
        out_shape=[pltpu.VMEM(shape, F32) for shape in shapes],
        compiler_params=SMALL,
        name="reference_products",
    )(*resident(own, mate, *currents))


def write_products(out, leads, followers):
    leads, followers = [[halves(a) for a in units] for units in (leads, followers)]
    out[0], out[1] = pairs_of(leads, followers)
    out[2] = joined([power(a) for a in leads])


def units_of(ref):
    return [ref[n // 2, n % 2] for n in range(4)]


def within_kernel(depth, *refs):
    chunks = len(refs) // (depth + 4)
    for n in range(chunks):
        got_ref, *cur_refs = refs[n * (depth + 1) : (n + 1) * (depth + 1)]
        lead_ref, seq_ref, pow_ref = refs[chunks * (depth + 1) + 3 * n :][:3]
        write_products(lead_ref, units_of(got_ref), units_of(cur_refs[0]))
        before = None
        for k, ref in enumerate(cur_refs):
            now = [halves(a) for a in units_of(ref)]
            pow_ref[k] = joined([power(a) for a in now])
            if k:
                seq_ref[k - 1, 0], seq_ref[k - 1, 1] = pairs_of(before, now)
            before = now


def within_products(got, currents):
    chunks, depth = len(currents), len(currents[0])
    _, _, columns, width = got[0].shape
    size = (columns // LOOK_RG, width // 2)
    arrays = [a for g, chunk in zip(got, currents) for a in (g, *chunk)]
    shapes = [(3, *size), (max(depth - 1, 1), 2, *size), (depth, *size)] * chunks
    outs = pl.pallas_call(
        partial(within_kernel, depth),
        in_specs=[VMEM] * len(arrays),
        out_specs=[VMEM] * len(shapes),
        out_shape=[pltpu.VMEM(shape, F32) for shape in shapes],
        compiler_params=SMALL,
        name="within_products",
    )(*resident(*arrays))
    return [outs[3 * n : 3 * n + 3] for n in range(chunks)]


def across_kernel(got_ref, first_ref, last_ref, out_ref):
    @pl.when(lax.axis_index("scene") & 1 == 1)
    def _():
        write_products(out_ref, units_of(last_ref), units_of(got_ref))

    @pl.when(lax.axis_index("scene") & 1 == 0)
    def _():
        write_products(out_ref, units_of(got_ref), units_of(first_ref))


def across_products(got, first, last):
    _, _, columns, width = got.shape
    return pl.pallas_call(
        across_kernel,
        in_specs=[VMEM] * 3,
        out_specs=VMEM,
        out_shape=pltpu.VMEM((3, columns // LOOK_RG, width // 2), F32),
        compiler_params=SMALL,
        name="across_products",
    )(*resident(got, first, last))


def pick_kernel(odd_ref, even_ref, out_ref):
    out_ref[...] = jnp.where(lax.axis_index("scene") & 1 == 1, odd_ref[...], even_ref[...])


def pick(odd, even):
    return pl.pallas_call(
        pick_kernel,
        in_specs=[VMEM] * 2,
        out_specs=VMEM,
        out_shape=pltpu.VMEM(odd.shape, odd.dtype),
        compiler_params=SMALL,
        name="pick",
    )(*resident(odd, even))


def finish_kernel(*refs):
    inputs, (ref_out, seq_out, coh_out) = refs[:-3], refs[-3:]
    at_head, odd = lax.axis_index("scene") == 0, lax.axis_index("scene") & 1 == 1
    lanes = inputs[1].shape[-1]
    for chunk in range(len(inputs) // 6):
        pairs, pair_pow, across, within, seq, powers = inputs[6 * chunk : 6 * chunk + 6]
        rows = slice(chunk * lanes, (chunk + 1) * lanes)

        def lead(place, own):
            return jnp.where(at_head, own, jnp.where(odd, within[place], across[place]))

        earlier = lead(2, pair_pow[...])
        for k in range(ref_out.shape[0]):
            if k:
                re, im = seq[k - 1, 0], seq[k - 1, 1]
            else:
                re, im = (lead(place, pairs[0, place]) for place in range(2))
            now = powers[k]
            ref_out[k, 0, :, rows] = pairs[k, 0]
            ref_out[k, 1, :, rows] = pairs[k, 1]
            seq_out[k, 0, :, rows] = re
            seq_out[k, 1, :, rows] = im
            coh_out[k, :, rows] = jnp.sqrt(re * re + im * im) / jnp.sqrt(earlier * now + eps_power)
            earlier = now


def finish(results, depth):
    flat = [a for result in results for a in result]
    blocks, lanes = flat[1].shape
    rows = len(results) * lanes
    shapes = [(depth, 2, blocks, rows)] * 2 + [(depth, blocks, rows)]
    outs = pl.pallas_call(
        finish_kernel,
        in_specs=[VMEM] * len(flat),
        out_specs=[VMEM] * 3,
        out_shape=[jax.ShapeDtypeStruct(shape, F32) for shape in shapes],
        compiler_params=SMALL,
        name="finish",
    )(*resident(*flat))
    return tuple(jnp.swapaxes(a, -1, -2) for a in outs)


def swapped(block, axis, bit):
    return lax.ppermute(block, axis, [(i, i ^ (1 << bit)) for i in range(lax.axis_size(axis))])


def neighbours(block, axis, first):
    count = lax.axis_size(axis)
    pairs = [(i, i + 1) for i in range(first, count - 1, 2)]
    return lax.ppermute(block, axis, pairs + [(j, i) for i, j in pairs])


def local(
    secondary,
    reference_store,
    tile_owner,
    az_kernel,
    rg_kernel,
    az_offset,
    az_index,
    rg_offset,
    rg_index,
):
    depth = secondary.shape[0]
    chunks = reference_store.shape[1] // 2
    bits = lax.axis_size("scene").bit_length() - 1

    arrived = swapped(reference_store, "scene", 0)
    operands, first, second = load(
        secondary, az_kernel.T, rg_kernel.T, rg_offset, rg_index, az_index, az_offset
    )
    first = neighbours(first, "range", 0)
    second = neighbours(second, "range", 1)
    stored, owner = (pltpu.with_memory_space_constraint(a, pltpu.HBM) for a in (reference_store, tile_owner))
    held = list(choose(owner, stored, arrived, 0, 0, chunks))
    for bit in range(1, bits):
        for n in range(chunks):
            got = swapped(held[n], "scene", bit)
            held[n] = choose(owner, held[n], got, n, bit, 1)[0]
    last = depth - 1
    early, late = [(last, 0), (0, 1)], [(k, n) for n in range(2) for k in range(depth)]
    late = [call for call in late if call not in early]
    units = dict(zip(early, resample(operands, first, second, early)))
    across = pick(units[last, 0], units[0, 1])
    across = neighbours(across, "scene", 1)
    units.update(zip(late, resample(operands, first, second, late)))
    currents = [[units[k, n] for k in range(depth)] for n in range(2)]
    within = []
    for n in range(2):
        within.append(swapped(currents[n][last], "scene", 0))
    within = within_products(within, currents)
    across = across_products(across, currents[0][0], currents[1][last])
    returned = neighbours(across, "scene", 1)
    results = []
    for n, small in enumerate(within):
        mate = swapped(held[n], "scene", 0)
        pairs, pair_pow = reference_products(held[n], mate, currents[n])
        results.append((pairs, pair_pow, (across, returned)[n], *small))
    return finish(results, depth)


def solution(mesh):
    in_specs = (
        P(("parts", "scene"), None, None, "range"),
        P(("parts", "scene"), None, None, None, "range"),
        P("parts"),
        P(),
        P(),
        P(("parts", "scene"), None),
        P(("parts", "scene"), None),
        P(("parts", "scene"), "range"),
        P(("parts", "scene"), "range"),
    )
    out_specs = (
        P(("parts", "scene"), None, None, "range"),
        P(("parts", "scene"), None, None, "range"),
        P(("parts", "scene"), None, "range"),
    )
    return jax.shard_map(local, mesh=mesh, in_specs=in_specs, out_specs=out_specs, check_vma=False)
```

```python
from functools import partial

import jax
import jax.numpy as jnp
from jax import lax
from jax.experimental import pallas as pl
from jax.experimental.pallas import tpu as pltpu
from jax.sharding import PartitionSpec as P


TILE = 256
LOOK_AZ = 4
LOOK_RG = 16

eps_power = 1e-06

BF = jnp.bfloat16
F32 = jnp.float32
ACROSS = (((1,), (0,)), ((), ()))
OVER_ROWS = (((0,), (0,)), ((), ()))
OVER_LANES = (((1,), (1,)), ((), ()))
VMEM = pl.BlockSpec(memory_space=pltpu.VMEM)
SMEM = pl.BlockSpec(memory_space=pltpu.SMEM)
SMALL = pltpu.CompilerParams(vmem_limit_bytes=12 << 20)


def iota(shape, dim):
    return lax.broadcasted_iota(jnp.int32, shape, dim)


def over(value, size):
    return value >> (size.bit_length() - 1)


def dot(a, b, dims=ACROSS):
    return lax.dot_general(a, b, dims, preferred_element_type=F32)


def lane_row(lane, half_rows):
    blocks = half_rows // LOOK_AZ
    inner = lane & (half_rows - 1)
    return LOOK_AZ * (inner & (blocks - 1)) + over(inner, blocks), over(lane, half_rows) & 1


def look_column(place, columns):
    blocks = columns // LOOK_RG
    return LOOK_RG * (place & (blocks - 1)) + over(place, blocks)


def chosen(shape, dim, wanted):
    return (iota(shape, dim) == wanted).astype(F32).astype(BF)


def taps_and_offsets(kernel_t, index_row, offset_row, spread):
    count = kernel_t.shape[1]
    taps = dot(kernel_t.astype(BF), chosen((count, index_row.shape[1]), 0, index_row))
    offsets = jnp.broadcast_to(offset_row.astype(F32), (8, offset_row.shape[1]))
    return dot(jnp.concatenate([taps, offsets], 0).astype(BF), spread)


def resident(*arrays):
    return [pltpu.with_memory_space_constraint(a, pltpu.VMEM) for a in arrays]


def load_kernel(margin, x_ref, *refs):
    count = (len(refs) - 4) // 2
    small_refs, x_out, outs = refs[:count], refs[count], refs[count + 1 : 2 * count + 1]
    first_ref, second_ref, sems = refs[2 * count + 1 :]
    depth, rows, parts, columns = x_ref.shape
    pieces = [(k, n) for k in range(depth) for n in range(rows // TILE)]

    def copy_of(position):
        k, n = pieces[position]
        size = TILE if n + 1 < rows // TILE else rows - n * TILE
        part = (k, pl.ds(n * TILE, size))
        return pltpu.make_async_copy(x_ref.at[part], x_out.at[part], sems.at[position]), part, size

    copies = [copy_of(position) for position in range(len(pieces))]
    small = [
        pltpu.make_async_copy(source, target, sems.at[len(pieces) + n])
        for n, (source, target) in enumerate(zip(small_refs, outs))
    ]
    for copy, _, _ in copies:
        copy.start()
    for copy in small:
        copy.start()
    place = iota((2 * margin, 1), 0)
    right_first = place + jnp.where(place < margin, columns - margin, -margin)
    left_first = place + jnp.where(place < margin, 0, columns - 2 * margin)
    edges = chosen((2 * margin, columns), 1, jnp.where(lax.axis_index("range") & 1 == 0, right_first, left_first))
    for (k, n), (copy, part, size) in zip(pieces, copies):
        copy.wait()
        found = dot(edges, x_out[part].reshape(parts * size, columns), OVER_LANES).astype(BF)
        lanes = slice(parts * n * TILE, parts * (n * TILE + size))
        first_ref[k, :, lanes] = found[:margin]
        second_ref[k, :, lanes] = found[margin:]
    for copy in small:
        copy.wait()


def load(secondary, *small):
    depth, rows, parts, _ = secondary.shape
    margin = (rows - small[-1].shape[1]) // 2
    operands = (secondary, *small)
    edge = pltpu.VMEM((depth, margin, parts * rows), BF)
    anywhere = pl.BlockSpec(memory_space=pl.ANY)
    outs = pl.pallas_call(
        partial(load_kernel, margin),
        in_specs=[anywhere] * len(operands),
        out_specs=[VMEM] * (len(operands) + 2),
        out_shape=[pltpu.VMEM(a.shape, a.dtype) for a in operands] + [edge, edge],
        scratch_shapes=[pltpu.SemaphoreType.DMA((depth * (rows // TILE) + len(small),))],
        compiler_params=SMALL,
        name="load",
    )(*[pltpu.with_memory_space_constraint(a, pltpu.HBM) for a in operands])
    return outs[:-2], outs[-2], outs[-1]


def range_matrix(margin, rows, kernel_ref, index_row, offset_row, order, column):
    taps = kernel_ref.shape[0]
    both = taps_and_offsets(kernel_ref[...], index_row, offset_row, order)
    base = column + both[taps : taps + 1].astype(jnp.int32) + (margin - 3)
    place = iota((taps, order.shape[1]), 0) - base
    value = tap_pattern(both, place & (taps - 1))
    blocks = [jnp.where(over(place + start, taps) == 0, value, 0.0) for start in range(0, rows, taps)]
    return jnp.concatenate(blocks, 0)


def tap_pattern(both, which):
    value = jnp.zeros(which.shape, F32)
    for tap in range(both.shape[0] - 8):
        value = jnp.where(which == tap, both[tap : tap + 1], value)
    return value


def azimuth_kernel(margin, x_ref, azk_ref, rgk_ref, rgo_ref, rgi_ref, azi_ref, azo_ref, z_ref, band_ref, rg_ref, spread_ref):
    depth, _, _, columns = x_ref.shape
    taps = azk_ref.shape[0]
    tile, lanes = spread_ref.shape
    half_rows, half_lanes = tile // 2, lanes // 2
    period = 2 * taps
    lane = iota((1, lanes), 1)
    row, part = lane_row(lane, half_rows)
    spread_ref[...] = chosen((tile, lanes), 0, row + half_rows * over(lane, half_lanes))
    column = look_column(iota((1, columns), 1), columns)
    order = chosen((columns, columns), 0, column)
    for k in range(depth):
        rg_ref[k] = range_matrix(
            margin, columns + 2 * margin, rgk_ref, rgi_ref[k : k + 1], rgo_ref[k : k + 1], order, column
        ).astype(BF)
    for k in range(depth):
        for s in range(z_ref.shape[1]):
            start = s * tile
            rows = slice(start, start + tile)
            both = taps_and_offsets(
                azk_ref[...], azi_ref[k : k + 1, rows], azo_ref[k : k + 1, rows], spread_ref[...]
            )
            base = row + both[taps : taps + 1].astype(jnp.int32) + (margin - 3)
            sub = iota((period, lanes), 0)
            place = (sub >> 1) - base
            value = tap_pattern(both, jnp.where((sub & 1) == part, place & (taps - 1), taps))
            home = -over(place, taps)
            for half in range(2):
                mine = slice(half * half_lanes, (half + 1) * half_lanes)
                band = band_ref.at[k, s, half]
                for block in range(band.shape[0] // period):
                    band[block * period : (block + 1) * period] = jnp.where(
                        home[:, mine] == block, value[:, mine], 0.0
                    ).astype(BF)
                begin = start + half * half_rows
                size = half_rows + 2 * margin
                window = x_ref[k, begin : begin + size].reshape(2 * size, columns)
                z_ref[k, s, half] = dot(window, band[...], OVER_ROWS).astype(BF)


def azimuth(operands, margin):
    depth, rows, parts, columns = operands[0].shape
    steps = (rows - 2 * margin) // TILE
    lanes = parts * TILE // 2
    shapes = [
        (depth, steps, 2, columns, lanes),
        (depth, steps, 2, parts * (TILE // 2 + 2 * margin), lanes),
        (depth, columns + 2 * margin, columns),
    ]
    return pl.pallas_call(
        partial(azimuth_kernel, margin),
        in_specs=[VMEM] * len(operands),
        out_specs=[VMEM] * len(shapes),
        out_shape=[pltpu.VMEM(shape, BF) for shape in shapes],
        scratch_shapes=[pltpu.VMEM((TILE, parts * TILE), BF)],
        compiler_params=SMALL,
        name="azimuth",
    )(*resident(*operands))


def range_kernel(calls, z_ref, band_ref, rg_ref, first_ref, second_ref, *outs):
    odd_column = lax.axis_index("range") & 1 == 1
    half_rows = z_ref.shape[4] // 2
    for out, (k, chunk) in zip(outs, calls):
        for s in range(2):
            for half in range(2):
                at = (k, 2 * chunk + s, half)
                begin = 2 * (2 * (2 * chunk + s) + half) * half_rows
                across = slice(begin, begin + band_ref.shape[3])
                first_side, second_side = first_ref[k, :, across], second_ref[k, :, across]
                wide = jnp.concatenate(
                    [
                        dot(jnp.where(odd_column, first_side, second_side), band_ref[at]).astype(BF),
                        z_ref[at],
                        dot(jnp.where(odd_column, second_side, first_side), band_ref[at]).astype(BF),
                    ],
                    0,
                )
                out[s, half] = dot(rg_ref[k], wide, OVER_ROWS).astype(BF)


def range_resample(azimuth_outs, first, second, calls):
    _, _, _, columns, lanes = azimuth_outs[0].shape
    arrays = resident(*azimuth_outs, first, second)
    return pl.pallas_call(
        partial(range_kernel, calls),
        in_specs=[VMEM] * len(arrays),
        out_specs=[VMEM] * len(calls),
        out_shape=[pltpu.VMEM((2, 2, columns, lanes), BF)] * len(calls),
        compiler_params=SMALL,
        name="range_resample",
    )(*arrays)


def choose_kernel(first, bit, stored, owner_ref, *refs):
    sources, outs, sems = refs[:2], refs[2:-1], refs[-1]
    me = lax.axis_index("scene")
    copies = []
    for n, out in enumerate(outs):
        tile = 2 * (first + n) + (me & 1)
        here, there = [ref.at[0, tile] if stored else ref for ref in sources]
        same = ((owner_ref[tile] ^ me) >> bit) & 1 == 0
        copies.append(pltpu.make_async_copy(here, out, sems.at[n]))
        pl.when(same)(copies[n].start)
        pl.when(jnp.logical_not(same))(pltpu.make_async_copy(there, out, sems.at[n]).start)
    for copy in copies:
        copy.wait()


def choose(owner, here, there, first, bit, chunks):
    return pl.pallas_call(
        partial(choose_kernel, first, bit, here.ndim > 3),
        in_specs=[SMEM, VMEM, VMEM],
        out_specs=[VMEM] * chunks,
        out_shape=[pltpu.VMEM(here.shape[-3:], BF)] * chunks,
        scratch_shapes=[pltpu.SemaphoreType.DMA((chunks,))],
        compiler_params=SMALL,
        name="choose",
    )(owner, *resident(here, there))


def lines(ref, look):
    blocks, width = ref.shape[0] // LOOK_RG, ref.shape[1] // 2
    wide = ref[look * blocks : (look + 1) * blocks].astype(F32)
    return wide[:, :width], wide[:, width:]


def multilook(terms, *refs):
    totals = None
    for look in range(LOOK_RG):
        found = terms(*[lines(ref, look) for ref in refs])
        totals = found if totals is None else [a + b for a, b in zip(totals, found)]
    means = []
    for total in totals:
        shift = total.shape[1] // 2
        while shift >= total.shape[1] // LOOK_AZ:
            total = total + pltpu.roll(total, shift, 1)
            shift //= 2
        means.append(total * (1.0 / (LOOK_AZ * LOOK_RG)))
    return means


def pair(first, second):
    a_re, a_im = first
    b_re, b_im = second
    return [a_re * b_re + a_im * b_im, a_im * b_re - a_re * b_im]


def power(first):
    re, im = first
    return [re * re + im * im]


def joined(pieces):
    blocks = pieces[0].shape[1] // LOOK_AZ
    group = over(iota(pieces[0].shape, 1), blocks)
    total = pieces[0]
    for position in range(1, len(pieces)):
        total = jnp.where(group >= position, pieces[position], total)
    return total


def gathered(units):
    return [joined(list(pieces)) for pieces in zip(*units)]


def reference_kernel(own_ref, mate_ref, *refs):
    depth = len(refs) - 3
    cur_refs, (pair_ref, pow_ref, lead_ref) = refs[:depth], refs[depth:]
    columns, half_rows = own_ref.shape[2], own_ref.shape[0] // 2
    core = lax.axis_index("scene") & 1
    size = 2 * half_rows
    row, part = lane_row(iota((1, size), 1), half_rows)
    order = chosen((size, size), 0, 2 * row + part)
    turn = chosen((columns, columns), 1, look_column(iota((columns, 1), 0), columns))

    def terms(lead, *currents):
        return power(lead) + [a for current in currents for a in pair(lead, current)]

    units = []
    for n, (ref, place) in enumerate(((own_ref, core), (mate_ref, 1 - core))):
        for half in range(2):
            rows = ref[half * half_rows : (half + 1) * half_rows].reshape(size, columns)
            lead_ref[2 * n + half] = dot(turn, dot(rows, order, OVER_ROWS).astype(BF)).astype(BF)
            units.append(
                multilook(terms, lead_ref.at[2 * n + half], *[ref.at[place, half] for ref in cur_refs])
            )
    units = [[jnp.where(core == 0, a, b) for a, b in zip(units[n], units[(n + 2) % 4])] for n in range(4)]
    pow_ref[...], *pairs = gathered(units)
    for n, found in enumerate(pairs):
        pair_ref[n // 2, n % 2] = found


def reference_products(own, mate, currents):
    _, _, columns, width = currents[0].shape
    depth = len(currents)
    shapes = [(depth, 2, columns // LOOK_RG, width // 2), (columns // LOOK_RG, width // 2)]
    return pl.pallas_call(
        reference_kernel,
        in_specs=[VMEM] * (2 + depth),
        out_specs=[VMEM] * len(shapes),
        out_shape=[pltpu.VMEM(shape, F32) for shape in shapes],
        scratch_shapes=[pltpu.VMEM((4, columns, width), BF)],
        compiler_params=SMALL,
        name="reference_products",
    )(*resident(own, mate, *currents))


def units_of(ref):
    return [ref.at[n // 2, n % 2] for n in range(4)]


def within_kernel(depth, *refs):
    chunks = len(refs) // (depth + 4)

    def terms(*rows):
        return [a for row in rows for a in power(row)] + [
            a for k in range(len(rows) - 1) for a in pair(rows[k], rows[k + 1])
        ]

    for n in range(chunks):
        sources = refs[n * (depth + 1) : (n + 1) * (depth + 1)]
        lead_ref, seq_ref, pow_ref = refs[chunks * (depth + 1) + 3 * n :][:3]
        units = [multilook(terms, *unit) for unit in zip(*map(units_of, sources))]
        lead_ref[2], *found = gathered(units)
        for k in range(depth):
            pow_ref[k] = found[k]
        lead_ref[0], lead_ref[1], *pairs = found[depth:]
        for m, a in enumerate(pairs):
            seq_ref[m // 2, m % 2] = a


def within_products(got, currents):
    chunks, depth = len(currents), len(currents[0])
    _, _, columns, width = got[0].shape
    size = (columns // LOOK_RG, width // 2)
    arrays = [a for g, chunk in zip(got, currents) for a in (g, *chunk)]
    shapes = [(3, *size), (max(depth - 1, 1), 2, *size), (depth, *size)] * chunks
    outs = pl.pallas_call(
        partial(within_kernel, depth),
        in_specs=[VMEM] * len(arrays),
        out_specs=[VMEM] * len(shapes),
        out_shape=[pltpu.VMEM(shape, F32) for shape in shapes],
        compiler_params=SMALL,
        name="within_products",
    )(*resident(*arrays))
    return [outs[3 * n : 3 * n + 3] for n in range(chunks)]


def across_kernel(got_ref, first_ref, last_ref, out_ref):
    def products(leads, followers):
        units = [
            multilook(lambda a, b: pair(a, b) + power(a), *unit)
            for unit in zip(units_of(leads), units_of(followers))
        ]
        out_ref[0], out_ref[1], out_ref[2] = gathered(units)

    odd = lax.axis_index("scene") & 1 == 1
    pl.when(odd)(lambda: products(last_ref, got_ref))
    pl.when(jnp.logical_not(odd))(lambda: products(got_ref, first_ref))


def across_products(got, first, last):
    _, _, columns, width = got.shape
    return pl.pallas_call(
        across_kernel,
        in_specs=[VMEM] * 3,
        out_specs=VMEM,
        out_shape=pltpu.VMEM((3, columns // LOOK_RG, width // 2), F32),
        compiler_params=SMALL,
        name="across_products",
    )(*resident(got, first, last))


def pick_kernel(odd_ref, even_ref, out_ref):
    out_ref[...] = jnp.where(lax.axis_index("scene") & 1 == 1, odd_ref[...], even_ref[...])


def pick(odd, even):
    return pl.pallas_call(
        pick_kernel,
        in_specs=[VMEM] * 2,
        out_specs=VMEM,
        out_shape=pltpu.VMEM(odd.shape, odd.dtype),
        compiler_params=SMALL,
        name="pick",
    )(*resident(odd, even))


def finish_kernel(*refs):
    inputs, (ref_out, seq_out, coh_out) = refs[:-3], refs[-3:]
    at_head, odd = lax.axis_index("scene") == 0, lax.axis_index("scene") & 1 == 1
    lanes = inputs[1].shape[-1]
    for chunk in range(len(inputs) // 6):
        pairs, pair_pow, across, within, seq, powers = inputs[6 * chunk : 6 * chunk + 6]
        rows = slice(chunk * lanes, (chunk + 1) * lanes)

        def lead(place, own):
            return jnp.where(at_head, own, jnp.where(odd, within[place], across[place]))

        earlier = lead(2, pair_pow[...])
        for k in range(ref_out.shape[0]):
            if k:
                re, im = seq[k - 1, 0], seq[k - 1, 1]
            else:
                re, im = (lead(place, pairs[0, place]) for place in range(2))
            now = powers[k]
            ref_out[k, 0, :, rows] = pairs[k, 0]
            ref_out[k, 1, :, rows] = pairs[k, 1]
            seq_out[k, 0, :, rows] = re
            seq_out[k, 1, :, rows] = im
            coh_out[k, :, rows] = jnp.sqrt(re * re + im * im) / jnp.sqrt(earlier * now + eps_power)
            earlier = now


def finish(results, depth):
    flat = [a for result in results for a in result]
    blocks, lanes = flat[1].shape
    rows = len(results) * lanes
    shapes = [(depth, 2, blocks, rows)] * 2 + [(depth, blocks, rows)]
    outs = pl.pallas_call(
        finish_kernel,
        in_specs=[VMEM] * len(flat),
        out_specs=[VMEM] * 3,
        out_shape=[jax.ShapeDtypeStruct(shape, F32) for shape in shapes],
        compiler_params=SMALL,
        name="finish",
    )(*resident(*flat))
    return tuple(jnp.swapaxes(a, -1, -2) for a in outs)


def swapped(block, axis, bit):
    return lax.ppermute(block, axis, [(i, i ^ (1 << bit)) for i in range(lax.axis_size(axis))])


def neighbours(block, axis, first, around=False):
    count = lax.axis_size(axis)
    pairs = [(i, (i + 1) % count) for i in range(first, count - 1 + around, 2)]
    return lax.ppermute(block, axis, pairs + [(j, i) for i, j in pairs])


def local(
    secondary,
    reference_store,
    tile_owner,
    az_kernel,
    rg_kernel,
    az_offset,
    az_index,
    rg_offset,
    rg_index,
):
    depth = secondary.shape[0]
    chunks = reference_store.shape[1] // 2
    bits = lax.axis_size("scene").bit_length() - 1

    arrived = swapped(reference_store, "scene", 0)
    operands, first, second = load(
        secondary, reference_store, az_kernel.T, rg_kernel.T, rg_offset, rg_index, az_index, az_offset
    )
    secondary, stored, *tables = operands
    operands = (secondary, *tables)
    owner = pltpu.with_memory_space_constraint(tile_owner, pltpu.HBM)
    held = list(choose(owner, stored, arrived, 0, 0, chunks))
    for bit in range(1, bits):
        for n in range(chunks):
            got = swapped(held[n], "scene", bit)
            held[n] = choose(owner, held[n], got, n, bit, 1)[0]
    turned = azimuth(operands, first.shape[1])
    first = neighbours(first, "range", 0)
    second = neighbours(second, "range", 1)
    last = depth - 1
    early, late = [(last, 0), (0, 1)], [(k, n) for n in range(2) for k in range(depth)]
    late = [call for call in late if call not in early]
    units = dict(zip(early, range_resample(turned, first, second, early)))
    across = pick(units[last, 0], units[0, 1])
    across = neighbours(across, "scene", 1)
    units.update(zip(late, range_resample(turned, first, second, late)))
    currents = [[units[k, n] for k in range(depth)] for n in range(2)]
    within = []
    for n in range(2):
        within.append(swapped(currents[n][last], "scene", 0))
    within = within_products(within, currents)
    across = across_products(across, currents[0][0], currents[1][last])
    returned = neighbours(across, "scene", 1, True)
    results = []
    for n, small in enumerate(within):
        mate = swapped(held[n], "scene", 0)
        pairs, pair_pow = reference_products(held[n], mate, currents[n])
        results.append((pairs, pair_pow, (across, returned)[n], *small))
    return finish(results, depth)


def solution(mesh):
    in_specs = (
        P(("parts", "scene"), None, None, "range"),
        P(("parts", "scene"), None, None, None, "range"),
        P("parts"),
        P(),
        P(),
        P(("parts", "scene"), None),
        P(("parts", "scene"), None),
        P(("parts", "scene"), "range"),
        P(("parts", "scene"), "range"),
    )
    out_specs = (
        P(("parts", "scene"), None, None, "range"),
        P(("parts", "scene"), None, None, "range"),
        P(("parts", "scene"), None, "range"),
    )
    return jax.shard_map(local, mesh=mesh, in_specs=in_specs, out_specs=out_specs, check_vma=False)
```

```python
from functools import partial

import jax
import jax.numpy as jnp
from jax import lax
from jax.experimental import pallas as pl
from jax.experimental.pallas import tpu as pltpu
from jax.sharding import PartitionSpec as P


TILE = 256
LOOK_AZ = 4
LOOK_RG = 16

eps_power = 1e-06

BF = jnp.bfloat16
F32 = jnp.float32
ACROSS = (((1,), (0,)), ((), ()))
OVER_ROWS = (((0,), (0,)), ((), ()))
OVER_LANES = (((1,), (1,)), ((), ()))
VMEM = pl.BlockSpec(memory_space=pltpu.VMEM)
SMEM = pl.BlockSpec(memory_space=pltpu.SMEM)
SMALL = pltpu.CompilerParams(vmem_limit_bytes=12 << 20)


def iota(shape, dim):
    return lax.broadcasted_iota(jnp.int32, shape, dim)


def over(value, size):
    return value >> (size.bit_length() - 1)


def dot(a, b, dims=ACROSS):
    return lax.dot_general(a, b, dims, preferred_element_type=F32)


def lane_row(lane, half_rows):
    blocks = half_rows // LOOK_AZ
    inner = lane & (half_rows - 1)
    return LOOK_AZ * (inner & (blocks - 1)) + over(inner, blocks), over(lane, half_rows) & 1


def look_column(place, columns):
    blocks = columns // LOOK_RG
    return LOOK_RG * (place & (blocks - 1)) + over(place, blocks)


def chosen(shape, dim, wanted):
    return (iota(shape, dim) == wanted).astype(F32).astype(BF)


def taps_and_offsets(kernel_t, index_row, offset_row, spread):
    count = kernel_t.shape[1]
    taps = dot(kernel_t.astype(BF), chosen((count, index_row.shape[1]), 0, index_row))
    offsets = jnp.broadcast_to(offset_row.astype(F32), (8, offset_row.shape[1]))
    return dot(jnp.concatenate([taps, offsets], 0).astype(BF), spread)


def resident(*arrays):
    return [pltpu.with_memory_space_constraint(a, pltpu.VMEM) for a in arrays]


def load_kernel(margin, x_ref, *refs):
    count = (len(refs) - 4) // 2
    small_refs, x_out, outs = refs[:count], refs[count], refs[count + 1 : 2 * count + 1]
    first_ref, second_ref, sems = refs[2 * count + 1 :]
    depth, rows, parts, columns = x_ref.shape
    pieces = [(k, n) for k in range(depth) for n in range(rows // TILE)]

    def copy_of(position):
        k, n = pieces[position]
        size = TILE if n + 1 < rows // TILE else rows - n * TILE
        part = (k, pl.ds(n * TILE, size))
        return pltpu.make_async_copy(x_ref.at[part], x_out.at[part], sems.at[position]), part, size

    copies = [copy_of(position) for position in range(len(pieces))]
    small = [
        pltpu.make_async_copy(source, target, sems.at[len(pieces) + n])
        for n, (source, target) in enumerate(zip(small_refs, outs))
    ]
    for copy, _, _ in copies:
        copy.start()
    for copy in small:
        copy.start()
    place = iota((2 * margin, 1), 0)
    right_first = place + jnp.where(place < margin, columns - margin, -margin)
    left_first = place + jnp.where(place < margin, 0, columns - 2 * margin)
    edges = chosen((2 * margin, columns), 1, jnp.where(lax.axis_index("range") & 1 == 0, right_first, left_first))
    for (k, n), (copy, part, size) in zip(pieces, copies):
        copy.wait()
        found = dot(edges, x_out[part].reshape(parts * size, columns), OVER_LANES).astype(BF)
        lanes = slice(parts * n * TILE, parts * (n * TILE + size))
        first_ref[k, :, lanes] = found[:margin]
        second_ref[k, :, lanes] = found[margin:]
    for copy in small:
        copy.wait()


def load(secondary, *small):
    depth, rows, parts, _ = secondary.shape
    margin = (rows - small[-1].shape[1]) // 2
    operands = (secondary, *small)
    edge = pltpu.VMEM((depth, margin, parts * rows), BF)
    anywhere = pl.BlockSpec(memory_space=pl.ANY)
    outs = pl.pallas_call(
        partial(load_kernel, margin),
        in_specs=[anywhere] * len(operands),
        out_specs=[VMEM] * (len(operands) + 2),
        out_shape=[pltpu.VMEM(a.shape, a.dtype) for a in operands] + [edge, edge],
        scratch_shapes=[pltpu.SemaphoreType.DMA((depth * (rows // TILE) + len(small),))],
        compiler_params=SMALL,
        name="load",
    )(*[pltpu.with_memory_space_constraint(a, pltpu.HBM) for a in operands])
    return outs[:-2], outs[-2], outs[-1]


def range_matrix(margin, rows, kernel_ref, index_row, offset_row, order, column):
    taps = kernel_ref.shape[0]
    both = taps_and_offsets(kernel_ref[...], index_row, offset_row, order)
    base = column + both[taps : taps + 1].astype(jnp.int32) + (margin - 3)
    place = iota((taps, order.shape[1]), 0) - base
    value = tap_pattern(both, place & (taps - 1))
    blocks = [jnp.where(over(place + start, taps) == 0, value, 0.0) for start in range(0, rows, taps)]
    return jnp.concatenate(blocks, 0)


def tap_pattern(both, which):
    value = jnp.zeros(which.shape, F32)
    for tap in range(both.shape[0] - 8):
        value = jnp.where(which == tap, both[tap : tap + 1], value)
    return value


def azimuth_kernel(margin, x_ref, azk_ref, rgk_ref, rgo_ref, rgi_ref, azi_ref, azo_ref, z_ref, band_ref, rg_ref, spread_ref):
    depth, _, _, columns = x_ref.shape
    taps = azk_ref.shape[0]
    tile, lanes = spread_ref.shape
    half_rows, half_lanes = tile // 2, lanes // 2
    period = 2 * taps
    lane = iota((1, lanes), 1)
    row, part = lane_row(lane, half_rows)
    spread_ref[...] = chosen((tile, lanes), 0, row + half_rows * over(lane, half_lanes))
    column = look_column(iota((1, columns), 1), columns)
    order = chosen((columns, columns), 0, column)
    for k in range(depth):
        rg_ref[k] = range_matrix(
            margin, columns + 2 * margin, rgk_ref, rgi_ref[k : k + 1], rgo_ref[k : k + 1], order, column
        ).astype(BF)
    for k in range(depth):
        for s in range(z_ref.shape[1]):
            start = s * tile
            rows = slice(start, start + tile)
            both = taps_and_offsets(
                azk_ref[...], azi_ref[k : k + 1, rows], azo_ref[k : k + 1, rows], spread_ref[...]
            )
            base = row + both[taps : taps + 1].astype(jnp.int32) + (margin - 3)
            sub = iota((period, lanes), 0)
            place = (sub >> 1) - base
            value = tap_pattern(both, jnp.where((sub & 1) == part, place & (taps - 1), taps))
            home = -over(place, taps)
            for half in range(2):
                mine = slice(half * half_lanes, (half + 1) * half_lanes)
                band = band_ref.at[k, s, half]
                for block in range(band.shape[0] // period):
                    band[block * period : (block + 1) * period] = jnp.where(
                        home[:, mine] == block, value[:, mine], 0.0
                    ).astype(BF)
                begin = start + half * half_rows
                size = half_rows + 2 * margin
                window = x_ref[k, begin : begin + size].reshape(2 * size, columns)
                z_ref[k, s, half] = dot(window, band[...], OVER_ROWS).astype(BF)


def azimuth(operands, margin):
    depth, rows, parts, columns = operands[0].shape
    steps = (rows - 2 * margin) // TILE
    lanes = parts * TILE // 2
    shapes = [
        (depth, steps, 2, columns, lanes),
        (depth, steps, 2, parts * (TILE // 2 + 2 * margin), lanes),
        (depth, columns + 2 * margin, columns),
    ]
    return pl.pallas_call(
        partial(azimuth_kernel, margin),
        in_specs=[VMEM] * len(operands),
        out_specs=[VMEM] * len(shapes),
        out_shape=[pltpu.VMEM(shape, BF) for shape in shapes],
        scratch_shapes=[pltpu.VMEM((TILE, parts * TILE), BF)],
        compiler_params=SMALL,
        name="azimuth",
    )(*resident(*operands))


def range_kernel(calls, z_ref, band_ref, rg_ref, first_ref, second_ref, *outs):
    odd_column = lax.axis_index("range") & 1 == 1
    half_rows = z_ref.shape[4] // 2
    for out, (k, chunk) in zip(outs, calls):
        for s in range(2):
            for half in range(2):
                at = (k, 2 * chunk + s, half)
                begin = 2 * (2 * (2 * chunk + s) + half) * half_rows
                across = slice(begin, begin + band_ref.shape[3])
                first_side, second_side = first_ref[k, :, across], second_ref[k, :, across]
                wide = jnp.concatenate(
                    [
                        dot(jnp.where(odd_column, first_side, second_side), band_ref[at]).astype(BF),
                        z_ref[at],
                        dot(jnp.where(odd_column, second_side, first_side), band_ref[at]).astype(BF),
                    ],
                    0,
                )
                out[s, half] = dot(rg_ref[k], wide, OVER_ROWS).astype(BF)


def range_resample(azimuth_outs, first, second, calls):
    _, _, _, columns, lanes = azimuth_outs[0].shape
    arrays = resident(*azimuth_outs, first, second)
    return pl.pallas_call(
        partial(range_kernel, calls),
        in_specs=[VMEM] * len(arrays),
        out_specs=[VMEM] * len(calls),
        out_shape=[pltpu.VMEM((2, 2, columns, lanes), BF)] * len(calls),
        compiler_params=SMALL,
        name="range_resample",
    )(*arrays)


def choose_kernel(bit, owner_ref, here_ref, there_ref, out_ref, sems):
    me = lax.axis_index("scene")
    copies = []
    for n in range(out_ref.shape[0]):
        tile = 2 * n + (me & 1)
        here, there = [ref.at[0, tile] if len(ref.shape) > 4 else ref.at[n] for ref in (here_ref, there_ref)]
        same = ((owner_ref[tile] ^ me) >> bit) & 1 == 0
        copies.append(pltpu.make_async_copy(here, out_ref.at[n], sems.at[n]))
        pl.when(same)(copies[n].start)
        pl.when(jnp.logical_not(same))(pltpu.make_async_copy(there, out_ref.at[n], sems.at[n]).start)
    for copy in copies:
        copy.wait()


def choose(owner, here, there, bit, chunks):
    return pl.pallas_call(
        partial(choose_kernel, bit),
        in_specs=[SMEM, VMEM, VMEM],
        out_specs=VMEM,
        out_shape=pltpu.VMEM((chunks, *here.shape[-3:]), BF),
        scratch_shapes=[pltpu.SemaphoreType.DMA((chunks,))],
        compiler_params=SMALL,
        name="choose",
    )(owner, *resident(here, there))


def lines(ref, look):
    blocks, width = ref.shape[0] // LOOK_RG, ref.shape[1] // 2
    wide = ref[look * blocks : (look + 1) * blocks].astype(F32)
    return wide[:, :width], wide[:, width:]


def multilook(terms, *refs):
    totals = None
    for look in range(LOOK_RG):
        found = terms(*[lines(ref, look) for ref in refs])
        totals = found if totals is None else [a + b for a, b in zip(totals, found)]
    means = []
    for total in totals:
        shift = total.shape[1] // 2
        while shift >= total.shape[1] // LOOK_AZ:
            total = total + pltpu.roll(total, shift, 1)
            shift //= 2
        means.append(total * (1.0 / (LOOK_AZ * LOOK_RG)))
    return means


def pair(first, second):
    a_re, a_im = first
    b_re, b_im = second
    return [a_re * b_re + a_im * b_im, a_im * b_re - a_re * b_im]


def power(first):
    re, im = first
    return [re * re + im * im]


def joined(pieces):
    blocks = pieces[0].shape[1] // LOOK_AZ
    group = over(iota(pieces[0].shape, 1), blocks)
    total = pieces[0]
    for position in range(1, len(pieces)):
        total = jnp.where(group >= position, pieces[position], total)
    return total


def gathered(units):
    return [joined(list(pieces)) for pieces in zip(*units)]


def reference_kernel(chunk, own_ref, mate_ref, *refs):
    depth = len(refs) - 3
    cur_refs, (pair_ref, pow_ref, lead_ref) = refs[:depth], refs[depth:]
    columns, half_rows = own_ref.shape[3], own_ref.shape[1] // 2
    core = lax.axis_index("scene") & 1
    size = 2 * half_rows
    row, part = lane_row(iota((1, size), 1), half_rows)
    order = chosen((size, size), 0, 2 * row + part)
    turn = chosen((columns, columns), 1, look_column(iota((columns, 1), 0), columns))

    def terms(lead, *currents):
        return power(lead) + [a for current in currents for a in pair(lead, current)]

    units = []
    for n, (ref, place) in enumerate(((own_ref, core), (mate_ref, 1 - core))):
        for half in range(2):
            rows = ref[chunk, half * half_rows : (half + 1) * half_rows].reshape(size, columns)
            lead_ref[2 * n + half] = dot(turn, dot(rows, order, OVER_ROWS).astype(BF)).astype(BF)
            units.append(
                multilook(terms, lead_ref.at[2 * n + half], *[ref.at[place, half] for ref in cur_refs])
            )
    units = [[jnp.where(core == 0, a, b) for a, b in zip(units[n], units[(n + 2) % 4])] for n in range(4)]
    pow_ref[...], *pairs = gathered(units)
    for n, found in enumerate(pairs):
        pair_ref[n // 2, n % 2] = found


def reference_products(own, mate, currents, chunk):
    _, _, columns, width = currents[0].shape
    depth = len(currents)
    shapes = [(depth, 2, columns // LOOK_RG, width // 2), (columns // LOOK_RG, width // 2)]
    return pl.pallas_call(
        partial(reference_kernel, chunk),
        in_specs=[VMEM] * (2 + depth),
        out_specs=[VMEM] * len(shapes),
        out_shape=[pltpu.VMEM(shape, F32) for shape in shapes],
        scratch_shapes=[pltpu.VMEM((4, columns, width), BF)],
        compiler_params=SMALL,
        name="reference_products",
    )(*resident(own, mate, *currents))


def units_of(ref):
    return [ref.at[n // 2, n % 2] for n in range(4)]


def within_kernel(depth, *refs):
    chunks = len(refs) // (depth + 4)

    def terms(*rows):
        return [a for row in rows for a in power(row)] + [
            a for k in range(len(rows) - 1) for a in pair(rows[k], rows[k + 1])
        ]

    for n in range(chunks):
        sources = refs[n * (depth + 1) : (n + 1) * (depth + 1)]
        lead_ref, seq_ref, pow_ref = refs[chunks * (depth + 1) + 3 * n :][:3]
        units = [multilook(terms, *unit) for unit in zip(*map(units_of, sources))]
        lead_ref[2], *found = gathered(units)
        for k in range(depth):
            pow_ref[k] = found[k]
        lead_ref[0], lead_ref[1], *pairs = found[depth:]
        for m, a in enumerate(pairs):
            seq_ref[m // 2, m % 2] = a


def within_products(got, currents):
    chunks, depth = len(currents), len(currents[0])
    _, _, columns, width = got[0].shape
    size = (columns // LOOK_RG, width // 2)
    arrays = [a for g, chunk in zip(got, currents) for a in (g, *chunk)]
    shapes = [(3, *size), (max(depth - 1, 1), 2, *size), (depth, *size)] * chunks
    outs = pl.pallas_call(
        partial(within_kernel, depth),
        in_specs=[VMEM] * len(arrays),
        out_specs=[VMEM] * len(shapes),
        out_shape=[pltpu.VMEM(shape, F32) for shape in shapes],
        compiler_params=SMALL,
        name="within_products",
    )(*resident(*arrays))
    return [outs[3 * n : 3 * n + 3] for n in range(chunks)]


def across_kernel(got_ref, first_ref, last_ref, out_ref):
    def products(leads, followers):
        units = [
            multilook(lambda a, b: pair(a, b) + power(a), *unit)
            for unit in zip(units_of(leads), units_of(followers))
        ]
        out_ref[0], out_ref[1], out_ref[2] = gathered(units)

    odd = lax.axis_index("scene") & 1 == 1
    pl.when(odd)(lambda: products(last_ref, got_ref))
    pl.when(jnp.logical_not(odd))(lambda: products(got_ref, first_ref))


def across_products(got, first, last):
    _, _, columns, width = got.shape
    return pl.pallas_call(
        across_kernel,
        in_specs=[VMEM] * 3,
        out_specs=VMEM,
        out_shape=pltpu.VMEM((3, columns // LOOK_RG, width // 2), F32),
        compiler_params=SMALL,
        name="across_products",
    )(*resident(got, first, last))


def pick_kernel(odd_ref, even_ref, out_ref):
    out_ref[...] = jnp.where(lax.axis_index("scene") & 1 == 1, odd_ref[...], even_ref[...])


def pick(odd, even):
    return pl.pallas_call(
        pick_kernel,
        in_specs=[VMEM] * 2,
        out_specs=VMEM,
        out_shape=pltpu.VMEM(odd.shape, odd.dtype),
        compiler_params=SMALL,
        name="pick",
    )(*resident(odd, even))


def finish_kernel(*refs):
    inputs, (ref_out, seq_out, coh_out) = refs[:-3], refs[-3:]
    at_head, odd = lax.axis_index("scene") == 0, lax.axis_index("scene") & 1 == 1
    lanes = inputs[1].shape[-1]
    for chunk in range(len(inputs) // 6):
        pairs, pair_pow, across, within, seq, powers = inputs[6 * chunk : 6 * chunk + 6]
        rows = slice(chunk * lanes, (chunk + 1) * lanes)

        def lead(place, own):
            return jnp.where(at_head, own, jnp.where(odd, within[place], across[place]))

        earlier = lead(2, pair_pow[...])
        for k in range(ref_out.shape[0]):
            if k:
                re, im = seq[k - 1, 0], seq[k - 1, 1]
            else:
                re, im = (lead(place, pairs[0, place]) for place in range(2))
            now = powers[k]
            ref_out[k, 0, :, rows] = pairs[k, 0]
            ref_out[k, 1, :, rows] = pairs[k, 1]
            seq_out[k, 0, :, rows] = re
            seq_out[k, 1, :, rows] = im
            coh_out[k, :, rows] = jnp.sqrt(re * re + im * im) / jnp.sqrt(earlier * now + eps_power)
            earlier = now


def finish(results, depth):
    flat = [a for result in results for a in result]
    blocks, lanes = flat[1].shape
    rows = len(results) * lanes
    shapes = [(depth, 2, blocks, rows)] * 2 + [(depth, blocks, rows)]
    outs = pl.pallas_call(
        finish_kernel,
        in_specs=[VMEM] * len(flat),
        out_specs=[VMEM] * 3,
        out_shape=[jax.ShapeDtypeStruct(shape, F32) for shape in shapes],
        compiler_params=SMALL,
        name="finish",
    )(*resident(*flat))
    return tuple(jnp.swapaxes(a, -1, -2) for a in outs)


def swapped(block, axis, bit):
    return lax.ppermute(block, axis, [(i, i ^ (1 << bit)) for i in range(lax.axis_size(axis))])


def neighbours(block, axis, first, around=False):
    count = lax.axis_size(axis)
    pairs = [(i, (i + 1) % count) for i in range(first, count - 1 + around, 2)]
    return lax.ppermute(block, axis, pairs + [(j, i) for i, j in pairs])


def local(
    secondary,
    reference_store,
    tile_owner,
    az_kernel,
    rg_kernel,
    az_offset,
    az_index,
    rg_offset,
    rg_index,
):
    depth = secondary.shape[0]
    chunks = reference_store.shape[1] // 2
    bits = lax.axis_size("scene").bit_length() - 1

    arrived = swapped(reference_store, "scene", 0)
    operands, first, second = load(
        secondary, reference_store, az_kernel.T, rg_kernel.T, rg_offset, rg_index, az_index, az_offset
    )
    secondary, stored, *tables = operands
    operands = (secondary, *tables)
    owner = pltpu.with_memory_space_constraint(tile_owner, pltpu.HBM)
    held = choose(owner, stored, arrived, 0, chunks)
    for bit in range(1, bits):
        got = swapped(held, "scene", bit)
        held = choose(owner, held, got, bit, chunks)
    mate = swapped(held, "scene", 0)
    turned = azimuth(operands, first.shape[1])
    first = neighbours(first, "range", 0)
    second = neighbours(second, "range", 1)
    last = depth - 1
    early, late = [(last, 0), (0, 1)], [(k, n) for n in range(2) for k in range(depth)]
    late = [call for call in late if call not in early]
    units = dict(zip(early, range_resample(turned, first, second, early)))
    across = pick(units[last, 0], units[0, 1])
    across = neighbours(across, "scene", 1)
    units.update(zip(late, range_resample(turned, first, second, late)))
    currents = [[units[k, n] for k in range(depth)] for n in range(2)]
    within = []
    for n in range(2):
        within.append(swapped(currents[n][last], "scene", 0))
    within = within_products(within, currents)
    across = across_products(across, currents[0][0], currents[1][last])
    returned = neighbours(across, "scene", 1, True)
    results = []
    for n, small in enumerate(within):
        pairs, pair_pow = reference_products(held, mate, currents[n], n)
        results.append((pairs, pair_pow, (across, returned)[n], *small))
    return finish(results, depth)


def solution(mesh):
    in_specs = (
        P(("parts", "scene"), None, None, "range"),
        P(("parts", "scene"), None, None, None, "range"),
        P("parts"),
        P(),
        P(),
        P(("parts", "scene"), None),
        P(("parts", "scene"), None),
        P(("parts", "scene"), "range"),
        P(("parts", "scene"), "range"),
    )
    out_specs = (
        P(("parts", "scene"), None, None, "range"),
        P(("parts", "scene"), None, None, "range"),
        P(("parts", "scene"), None, "range"),
    )
    return jax.shard_map(local, mesh=mesh, in_specs=in_specs, out_specs=out_specs, check_vma=False)
```

```python
from functools import partial

import jax
import jax.numpy as jnp
from jax import lax
from jax.experimental import pallas as pl
from jax.experimental.pallas import tpu as pltpu
from jax.sharding import PartitionSpec as P


TILE = 256
LOOK_AZ = 4
LOOK_RG = 16

eps_power = 1e-06

BF = jnp.bfloat16
F32 = jnp.float32
ACROSS = (((1,), (0,)), ((), ()))
OVER_ROWS = (((0,), (0,)), ((), ()))
OVER_LANES = (((1,), (1,)), ((), ()))
VMEM = pl.BlockSpec(memory_space=pltpu.VMEM)
SMEM = pl.BlockSpec(memory_space=pltpu.SMEM)
SMALL = pltpu.CompilerParams(vmem_limit_bytes=12 << 20)


def iota(shape, dim):
    return lax.broadcasted_iota(jnp.int32, shape, dim)


def over(value, size):
    return value >> (size.bit_length() - 1)


def dot(a, b, dims=ACROSS):
    return lax.dot_general(a, b, dims, preferred_element_type=F32)


def lane_row(lane, half_rows):
    blocks = half_rows // LOOK_AZ
    inner = lane & (half_rows - 1)
    return LOOK_AZ * (inner & (blocks - 1)) + over(inner, blocks), over(lane, half_rows) & 1


def look_column(place, columns):
    blocks = columns // LOOK_RG
    return LOOK_RG * (place & (blocks - 1)) + over(place, blocks)


def chosen(shape, dim, wanted):
    return (iota(shape, dim) == wanted).astype(F32).astype(BF)


def taps_and_offsets(kernel_t, index_row, offset_row, spread):
    count = kernel_t.shape[1]
    taps = dot(kernel_t.astype(BF), chosen((count, index_row.shape[1]), 0, index_row))
    offsets = jnp.broadcast_to(offset_row.astype(F32), (8, offset_row.shape[1]))
    return dot(jnp.concatenate([taps, offsets], 0).astype(BF), spread)


def resident(*arrays):
    return [pltpu.with_memory_space_constraint(a, pltpu.VMEM) for a in arrays]


def load_kernel(margin, x_ref, *refs):
    count = (len(refs) - 4) // 2
    small_refs, x_out, outs = refs[:count], refs[count], refs[count + 1 : 2 * count + 1]
    first_ref, second_ref, sems = refs[2 * count + 1 :]
    depth, rows, parts, columns = x_ref.shape
    pieces = [(k, n) for k in range(depth) for n in range(rows // TILE)]

    def copy_of(position):
        k, n = pieces[position]
        size = TILE if n + 1 < rows // TILE else rows - n * TILE
        part = (k, pl.ds(n * TILE, size))
        return pltpu.make_async_copy(x_ref.at[part], x_out.at[part], sems.at[position]), part, size

    copies = [copy_of(position) for position in range(len(pieces))]
    small = [
        pltpu.make_async_copy(source, target, sems.at[len(pieces) + n])
        for n, (source, target) in enumerate(zip(small_refs, outs))
    ]
    for copy, _, _ in copies:
        copy.start()
    for copy in small:
        copy.start()
    place = iota((2 * margin, 1), 0)
    right_first = place + jnp.where(place < margin, columns - margin, -margin)
    left_first = place + jnp.where(place < margin, 0, columns - 2 * margin)
    edges = chosen((2 * margin, columns), 1, jnp.where(lax.axis_index("range") & 1 == 0, right_first, left_first))
    for (k, n), (copy, part, size) in zip(pieces, copies):
        copy.wait()
        found = dot(edges, x_out[part].reshape(parts * size, columns), OVER_LANES).astype(BF)
        lanes = slice(parts * n * TILE, parts * (n * TILE + size))
        first_ref[k, :, lanes] = found[:margin]
        second_ref[k, :, lanes] = found[margin:]
    for copy in small:
        copy.wait()


def load(secondary, *small):
    depth, rows, parts, _ = secondary.shape
    margin = (rows - small[-1].shape[1]) // 2
    operands = (secondary, *small)
    edge = pltpu.VMEM((depth, margin, parts * rows), BF)
    anywhere = pl.BlockSpec(memory_space=pl.ANY)
    outs = pl.pallas_call(
        partial(load_kernel, margin),
        in_specs=[anywhere] * len(operands),
        out_specs=[SMEM if a.ndim == 1 else VMEM for a in operands] + [VMEM] * 2,
        out_shape=[(pltpu.SMEM if a.ndim == 1 else pltpu.VMEM)(a.shape, a.dtype) for a in operands] + [edge, edge],
        scratch_shapes=[pltpu.SemaphoreType.DMA((depth * (rows // TILE) + len(small),))],
        compiler_params=SMALL,
        name="load",
    )(*[pltpu.with_memory_space_constraint(a, pltpu.HBM) for a in operands])
    return outs[:-2], outs[-2], outs[-1]


def range_matrix(margin, rows, kernel_ref, index_row, offset_row, order, column):
    taps = kernel_ref.shape[0]
    both = taps_and_offsets(kernel_ref[...], index_row, offset_row, order)
    base = column + both[taps : taps + 1].astype(jnp.int32) + (margin - 3)
    place = iota((taps, order.shape[1]), 0) - base
    value = tap_pattern(both, place & (taps - 1))
    blocks = [jnp.where(over(place + start, taps) == 0, value, 0.0) for start in range(0, rows, taps)]
    return jnp.concatenate(blocks, 0)


def tap_pattern(both, which):
    value = jnp.zeros(which.shape, F32)
    for tap in range(both.shape[0] - 8):
        value = jnp.where(which == tap, both[tap : tap + 1], value)
    return value


def azimuth_kernel(margin, x_ref, azk_ref, rgk_ref, rgo_ref, rgi_ref, azi_ref, azo_ref, z_ref, band_ref, rg_ref, spread_ref):
    depth, _, _, columns = x_ref.shape
    taps = azk_ref.shape[0]
    tile, lanes = spread_ref.shape
    half_rows, half_lanes = tile // 2, lanes // 2
    period = 2 * taps
    lane = iota((1, lanes), 1)
    row, part = lane_row(lane, half_rows)
    spread_ref[...] = chosen((tile, lanes), 0, row + half_rows * over(lane, half_lanes))
    column = look_column(iota((1, columns), 1), columns)
    order = chosen((columns, columns), 0, column)
    for k in range(depth):
        rg_ref[k] = range_matrix(
            margin, columns + 2 * margin, rgk_ref, rgi_ref[k : k + 1], rgo_ref[k : k + 1], order, column
        ).astype(BF)
    for k in range(depth):
        for s in range(z_ref.shape[1]):
            start = s * tile
            rows = slice(start, start + tile)
            both = taps_and_offsets(
                azk_ref[...], azi_ref[k : k + 1, rows], azo_ref[k : k + 1, rows], spread_ref[...]
            )
            base = row + both[taps : taps + 1].astype(jnp.int32) + (margin - 3)
            sub = iota((period, lanes), 0)
            place = (sub >> 1) - base
            value = tap_pattern(both, jnp.where((sub & 1) == part, place & (taps - 1), taps))
            home = -over(place, taps)
            for half in range(2):
                mine = slice(half * half_lanes, (half + 1) * half_lanes)
                band = band_ref.at[k, s, half]
                for block in range(band.shape[0] // period):
                    band[block * period : (block + 1) * period] = jnp.where(
                        home[:, mine] == block, value[:, mine], 0.0
                    ).astype(BF)
                begin = start + half * half_rows
                size = half_rows + 2 * margin
                window = x_ref[k, begin : begin + size].reshape(2 * size, columns)
                z_ref[k, s, half] = dot(window, band[...], OVER_ROWS).astype(BF)


def azimuth(operands, margin):
    depth, rows, parts, columns = operands[0].shape
    steps = (rows - 2 * margin) // TILE
    lanes = parts * TILE // 2
    shapes = [
        (depth, steps, 2, columns, lanes),
        (depth, steps, 2, parts * (TILE // 2 + 2 * margin), lanes),
        (depth, columns + 2 * margin, columns),
    ]
    return pl.pallas_call(
        partial(azimuth_kernel, margin),
        in_specs=[VMEM] * len(operands),
        out_specs=[VMEM] * len(shapes),
        out_shape=[pltpu.VMEM(shape, BF) for shape in shapes],
        scratch_shapes=[pltpu.VMEM((TILE, parts * TILE), BF)],
        compiler_params=SMALL,
        name="azimuth",
    )(*resident(*operands))


def range_kernel(calls, z_ref, band_ref, rg_ref, first_ref, second_ref, *outs):
    odd_column = lax.axis_index("range") & 1 == 1
    half_rows = z_ref.shape[4] // 2
    for out, (k, chunk) in zip(outs, calls):
        for s in range(2):
            for half in range(2):
                at = (k, 2 * chunk + s, half)
                begin = 2 * (2 * (2 * chunk + s) + half) * half_rows
                across = slice(begin, begin + band_ref.shape[3])
                first_side, second_side = first_ref[k, :, across], second_ref[k, :, across]
                wide = jnp.concatenate(
                    [
                        dot(jnp.where(odd_column, first_side, second_side), band_ref[at]).astype(BF),
                        z_ref[at],
                        dot(jnp.where(odd_column, second_side, first_side), band_ref[at]).astype(BF),
                    ],
                    0,
                )
                out[s, half] = dot(rg_ref[k], wide, OVER_ROWS).astype(BF)


def range_resample(azimuth_outs, first, second, calls):
    _, _, _, columns, lanes = azimuth_outs[0].shape
    arrays = resident(*azimuth_outs, first, second)
    return pl.pallas_call(
        partial(range_kernel, calls),
        in_specs=[VMEM] * len(arrays),
        out_specs=[VMEM] * len(calls),
        out_shape=[pltpu.VMEM((2, 2, columns, lanes), BF)] * len(calls),
        compiler_params=SMALL,
        name="range_resample",
    )(*arrays)


def choose_kernel(bit, owner_ref, here_ref, there_ref, out_ref, sems):
    me = lax.axis_index("scene")
    copies = []
    for n in range(out_ref.shape[0]):
        tile = 2 * n + (me & 1)
        here, there = [ref.at[0, tile] if len(ref.shape) > 4 else ref.at[n] for ref in (here_ref, there_ref)]
        same = ((owner_ref[tile] ^ me) >> bit) & 1 == 0
        copies.append(pltpu.make_async_copy(here, out_ref.at[n], sems.at[n]))
        pl.when(same)(copies[n].start)
        pl.when(jnp.logical_not(same))(pltpu.make_async_copy(there, out_ref.at[n], sems.at[n]).start)
    for copy in copies:
        copy.wait()


def choose(owner, here, there, bit, chunks):
    return pl.pallas_call(
        partial(choose_kernel, bit),
        in_specs=[SMEM, VMEM, VMEM],
        out_specs=VMEM,
        out_shape=pltpu.VMEM((chunks, *here.shape[-3:]), BF),
        scratch_shapes=[pltpu.SemaphoreType.DMA((chunks,))],
        compiler_params=SMALL,
        name="choose",
    )(owner, *resident(here, there))


def lines(ref, look):
    blocks, width = ref.shape[0] // LOOK_RG, ref.shape[1] // 2
    wide = ref[look * blocks : (look + 1) * blocks].astype(F32)
    return wide[:, :width], wide[:, width:]


def multilook(terms, *refs):
    totals = None
    for look in range(LOOK_RG):
        found = terms(*[lines(ref, look) for ref in refs])
        totals = found if totals is None else [a + b for a, b in zip(totals, found)]
    means = []
    for total in totals:
        shift = total.shape[1] // 2
        while shift >= total.shape[1] // LOOK_AZ:
            total = total + pltpu.roll(total, shift, 1)
            shift //= 2
        means.append(total * (1.0 / (LOOK_AZ * LOOK_RG)))
    return means


def pair(first, second):
    a_re, a_im = first
    b_re, b_im = second
    return [a_re * b_re + a_im * b_im, a_im * b_re - a_re * b_im]


def power(first):
    re, im = first
    return [re * re + im * im]


def joined(pieces):
    blocks = pieces[0].shape[1] // LOOK_AZ
    group = over(iota(pieces[0].shape, 1), blocks)
    total = pieces[0]
    for position in range(1, len(pieces)):
        total = jnp.where(group >= position, pieces[position], total)
    return total


def gathered(units):
    return [joined(list(pieces)) for pieces in zip(*units)]


def reference_kernel(chunk, own_ref, mate_ref, *refs):
    depth = len(refs) - 3
    cur_refs, (pair_ref, pow_ref, lead_ref) = refs[:depth], refs[depth:]
    columns, half_rows = own_ref.shape[3], own_ref.shape[1] // 2
    core = lax.axis_index("scene") & 1
    size = 2 * half_rows
    row, part = lane_row(iota((1, size), 1), half_rows)
    order = chosen((size, size), 0, 2 * row + part)
    turn = chosen((columns, columns), 1, look_column(iota((columns, 1), 0), columns))

    def terms(lead, *currents):
        return power(lead) + [a for current in currents for a in pair(lead, current)]

    units = []
    for n, (ref, place) in enumerate(((own_ref, core), (mate_ref, 1 - core))):
        for half in range(2):
            rows = ref[chunk, half * half_rows : (half + 1) * half_rows].reshape(size, columns)
            lead_ref[2 * n + half] = dot(turn, dot(rows, order, OVER_ROWS).astype(BF)).astype(BF)
            units.append(
                multilook(terms, lead_ref.at[2 * n + half], *[ref.at[place, half] for ref in cur_refs])
            )
    units = [[jnp.where(core == 0, a, b) for a, b in zip(units[n], units[(n + 2) % 4])] for n in range(4)]
    pow_ref[...], *pairs = gathered(units)
    for n, found in enumerate(pairs):
        pair_ref[n // 2, n % 2] = found


def reference_products(own, mate, currents, chunk):
    _, _, columns, width = currents[0].shape
    depth = len(currents)
    shapes = [(depth, 2, columns // LOOK_RG, width // 2), (columns // LOOK_RG, width // 2)]
    return pl.pallas_call(
        partial(reference_kernel, chunk),
        in_specs=[VMEM] * (2 + depth),
        out_specs=[VMEM] * len(shapes),
        out_shape=[pltpu.VMEM(shape, F32) for shape in shapes],
        scratch_shapes=[pltpu.VMEM((4, columns, width), BF)],
        compiler_params=SMALL,
        name="reference_products",
    )(*resident(own, mate, *currents))


def units_of(ref):
    return [ref.at[n // 2, n % 2] for n in range(4)]


def within_kernel(depth, *refs):
    chunks = len(refs) // (depth + 4)

    def terms(*rows):
        return [a for row in rows for a in power(row)] + [
            a for k in range(len(rows) - 1) for a in pair(rows[k], rows[k + 1])
        ]

    for n in range(chunks):
        sources = refs[n * (depth + 1) : (n + 1) * (depth + 1)]
        lead_ref, seq_ref, pow_ref = refs[chunks * (depth + 1) + 3 * n :][:3]
        units = [multilook(terms, *unit) for unit in zip(*map(units_of, sources))]
        lead_ref[2], *found = gathered(units)
        for k in range(depth):
            pow_ref[k] = found[k]
        lead_ref[0], lead_ref[1], *pairs = found[depth:]
        for m, a in enumerate(pairs):
            seq_ref[m // 2, m % 2] = a


def within_products(got, currents):
    chunks, depth = len(currents), len(currents[0])
    _, _, columns, width = got[0].shape
    size = (columns // LOOK_RG, width // 2)
    arrays = [a for g, chunk in zip(got, currents) for a in (g, *chunk)]
    shapes = [(3, *size), (max(depth - 1, 1), 2, *size), (depth, *size)] * chunks
    outs = pl.pallas_call(
        partial(within_kernel, depth),
        in_specs=[VMEM] * len(arrays),
        out_specs=[VMEM] * len(shapes),
        out_shape=[pltpu.VMEM(shape, F32) for shape in shapes],
        compiler_params=SMALL,
        name="within_products",
    )(*resident(*arrays))
    return [outs[3 * n : 3 * n + 3] for n in range(chunks)]


def across_kernel(got_ref, first_ref, last_ref, out_ref):
    def products(leads, followers):
        units = [
            multilook(lambda a, b: pair(a, b) + power(a), *unit)
            for unit in zip(units_of(leads), units_of(followers))
        ]
        out_ref[0], out_ref[1], out_ref[2] = gathered(units)

    odd = lax.axis_index("scene") & 1 == 1
    pl.when(odd)(lambda: products(last_ref, got_ref))
    pl.when(jnp.logical_not(odd))(lambda: products(got_ref, first_ref))


def across_products(got, first, last):
    _, _, columns, width = got.shape
    return pl.pallas_call(
        across_kernel,
        in_specs=[VMEM] * 3,
        out_specs=VMEM,
        out_shape=pltpu.VMEM((3, columns // LOOK_RG, width // 2), F32),
        compiler_params=SMALL,
        name="across_products",
    )(*resident(got, first, last))


def pick_kernel(odd_ref, even_ref, out_ref):
    out_ref[...] = jnp.where(lax.axis_index("scene") & 1 == 1, odd_ref[...], even_ref[...])


def pick(odd, even):
    return pl.pallas_call(
        pick_kernel,
        in_specs=[VMEM] * 2,
        out_specs=VMEM,
        out_shape=pltpu.VMEM(odd.shape, odd.dtype),
        compiler_params=SMALL,
        name="pick",
    )(*resident(odd, even))


def finish_kernel(*refs):
    inputs, (ref_out, seq_out, coh_out) = refs[:-3], refs[-3:]
    at_head, odd = lax.axis_index("scene") == 0, lax.axis_index("scene") & 1 == 1
    lanes = inputs[1].shape[-1]
    for chunk in range(len(inputs) // 6):
        pairs, pair_pow, across, within, seq, powers = inputs[6 * chunk : 6 * chunk + 6]
        rows = slice(chunk * lanes, (chunk + 1) * lanes)

        def lead(place, own):
            return jnp.where(at_head, own, jnp.where(odd, within[place], across[place]))

        earlier = lead(2, pair_pow[...])
        for k in range(ref_out.shape[0]):
            if k:
                re, im = seq[k - 1, 0], seq[k - 1, 1]
            else:
                re, im = (lead(place, pairs[0, place]) for place in range(2))
            now = powers[k]
            ref_out[k, 0, :, rows] = pairs[k, 0]
            ref_out[k, 1, :, rows] = pairs[k, 1]
            seq_out[k, 0, :, rows] = re
            seq_out[k, 1, :, rows] = im
            coh_out[k, :, rows] = jnp.sqrt(re * re + im * im) / jnp.sqrt(earlier * now + eps_power)
            earlier = now


def finish(results, depth):
    flat = [a for result in results for a in result]
    blocks, lanes = flat[1].shape
    rows = len(results) * lanes
    shapes = [(depth, 2, blocks, rows)] * 2 + [(depth, blocks, rows)]
    outs = pl.pallas_call(
        finish_kernel,
        in_specs=[VMEM] * len(flat),
        out_specs=[VMEM] * 3,
        out_shape=[jax.ShapeDtypeStruct(shape, F32) for shape in shapes],
        compiler_params=SMALL,
        name="finish",
    )(*resident(*flat))
    return tuple(jnp.swapaxes(a, -1, -2) for a in outs)


def swapped(block, axis, bit):
    return lax.ppermute(block, axis, [(i, i ^ (1 << bit)) for i in range(lax.axis_size(axis))])


def neighbours(block, axis, first, around=False):
    count = lax.axis_size(axis)
    pairs = [(i, (i + 1) % count) for i in range(first, count - 1 + around, 2)]
    return lax.ppermute(block, axis, pairs + [(j, i) for i, j in pairs])


def local(
    secondary,
    reference_store,
    tile_owner,
    az_kernel,
    rg_kernel,
    az_offset,
    az_index,
    rg_offset,
    rg_index,
):
    depth = secondary.shape[0]
    chunks = reference_store.shape[1] // 2
    bits = lax.axis_size("scene").bit_length() - 1

    arrived = swapped(reference_store, "scene", 0)
    operands, first, second = load(
        secondary, tile_owner, reference_store, az_kernel.T, rg_kernel.T, rg_offset, rg_index, az_index, az_offset
    )
    secondary, owner, stored, *tables = operands
    operands = (secondary, *tables)
    owner = pltpu.with_memory_space_constraint(owner, pltpu.SMEM)
    held = choose(owner, stored, arrived, 0, chunks)
    for bit in range(1, bits):
        got = swapped(held, "scene", bit)
        held = choose(owner, held, got, bit, chunks)
    mate = swapped(held, "scene", 0)
    turned = azimuth(operands, first.shape[1])
    first = neighbours(first, "range", 0)
    second = neighbours(second, "range", 1)
    last = depth - 1
    early, late = [(last, 0), (0, 1)], [(k, n) for n in range(2) for k in range(depth)]
    late = [call for call in late if call not in early]
    units = dict(zip(early, range_resample(turned, first, second, early)))
    across = pick(units[last, 0], units[0, 1])
    across = neighbours(across, "scene", 1)
    units.update(zip(late, range_resample(turned, first, second, late)))
    currents = [[units[k, n] for k in range(depth)] for n in range(2)]
    within = []
    for n in range(2):
        within.append(swapped(currents[n][last], "scene", 0))
    within = within_products(within, currents)
    across = across_products(across, currents[0][0], currents[1][last])
    returned = neighbours(across, "scene", 1, True)
    results = []
    for n, small in enumerate(within):
        pairs, pair_pow = reference_products(held, mate, currents[n], n)
        results.append((pairs, pair_pow, (across, returned)[n], *small))
    return finish(results, depth)


def solution(mesh):
    in_specs = (
        P(("parts", "scene"), None, None, "range"),
        P(("parts", "scene"), None, None, None, "range"),
        P("parts"),
        P(),
        P(),
        P(("parts", "scene"), None),
        P(("parts", "scene"), None),
        P(("parts", "scene"), "range"),
        P(("parts", "scene"), "range"),
    )
    out_specs = (
        P(("parts", "scene"), None, None, "range"),
        P(("parts", "scene"), None, None, "range"),
        P(("parts", "scene"), None, "range"),
    )
    return jax.shard_map(local, mesh=mesh, in_specs=in_specs, out_specs=out_specs, check_vma=False)
```

```python
from functools import partial

import jax
import jax.numpy as jnp
from jax import lax
from jax.experimental import pallas as pl
from jax.experimental.pallas import tpu as pltpu
from jax.sharding import PartitionSpec as P


TILE = 256
LOOK_AZ = 4
LOOK_RG = 16

eps_power = 1e-06

BF = jnp.bfloat16
F32 = jnp.float32
ACROSS = (((1,), (0,)), ((), ()))
OVER_ROWS = (((0,), (0,)), ((), ()))
OVER_LANES = (((1,), (1,)), ((), ()))
VMEM = pl.BlockSpec(memory_space=pltpu.VMEM)
SMEM = pl.BlockSpec(memory_space=pltpu.SMEM)
SMALL = pltpu.CompilerParams(vmem_limit_bytes=12 << 20)


def iota(shape, dim):
    return lax.broadcasted_iota(jnp.int32, shape, dim)


def over(value, size):
    return value >> (size.bit_length() - 1)


def dot(a, b, dims=ACROSS):
    return lax.dot_general(a, b, dims, preferred_element_type=F32)


def lane_row(lane, half_rows):
    blocks = half_rows // LOOK_AZ
    inner = lane & (half_rows - 1)
    return LOOK_AZ * (inner & (blocks - 1)) + over(inner, blocks), over(lane, half_rows) & 1


def look_column(place, columns):
    blocks = columns // LOOK_RG
    return LOOK_RG * (place & (blocks - 1)) + over(place, blocks)


def chosen(shape, dim, wanted):
    return (iota(shape, dim) == wanted).astype(F32).astype(BF)


def taps_and_offsets(kernel_t, index_row, offset_row, spread):
    count = kernel_t.shape[1]
    taps = dot(kernel_t.astype(BF), chosen((count, index_row.shape[1]), 0, index_row))
    offsets = jnp.broadcast_to(offset_row.astype(F32), (8, offset_row.shape[1]))
    return dot(jnp.concatenate([taps, offsets], 0).astype(BF), spread)


def resident(*arrays):
    return [pltpu.with_memory_space_constraint(a, pltpu.VMEM) for a in arrays]


def load_kernel(margin, x_ref, *refs):
    count = (len(refs) - 4) // 2
    small_refs, x_out, outs = refs[:count], refs[count], refs[count + 1 : 2 * count + 1]
    first_ref, second_ref, sems = refs[2 * count + 1 :]
    depth, rows, parts, columns = x_ref.shape
    pieces = [(k, n) for k in range(depth) for n in range(rows // TILE)]

    def copy_of(position):
        k, n = pieces[position]
        size = TILE if n + 1 < rows // TILE else rows - n * TILE
        part = (k, pl.ds(n * TILE, size))
        return pltpu.make_async_copy(x_ref.at[part], x_out.at[part], sems.at[position]), part, size

    copies = [copy_of(position) for position in range(len(pieces))]
    small = [
        pltpu.make_async_copy(source, target, sems.at[len(pieces) + n])
        for n, (source, target) in enumerate(zip(small_refs, outs))
    ]
    for copy, _, _ in copies:
        copy.start()
    for copy in small:
        copy.start()
    place = iota((2 * margin, 1), 0)
    right_first = place + jnp.where(place < margin, columns - margin, -margin)
    left_first = place + jnp.where(place < margin, 0, columns - 2 * margin)
    edges = chosen((2 * margin, columns), 1, jnp.where(lax.axis_index("range") & 1 == 0, right_first, left_first))
    for (k, n), (copy, part, size) in zip(pieces, copies):
        copy.wait()
        found = dot(edges, x_out[part].reshape(parts * size, columns), OVER_LANES).astype(BF)
        lanes = slice(parts * n * TILE, parts * (n * TILE + size))
        first_ref[k, :, lanes] = found[:margin]
        second_ref[k, :, lanes] = found[margin:]
    for copy in small:
        copy.wait()


def load(secondary, *small):
    depth, rows, parts, _ = secondary.shape
    margin = (rows - small[-1].shape[1]) // 2
    operands = (secondary, *small)
    edge = pltpu.VMEM((depth, margin, parts * rows), BF)
    anywhere = pl.BlockSpec(memory_space=pl.ANY)
    outs = pl.pallas_call(
        partial(load_kernel, margin),
        in_specs=[anywhere] * len(operands),
        out_specs=[SMEM if a.ndim == 1 else VMEM for a in operands] + [VMEM] * 2,
        out_shape=[(pltpu.SMEM if a.ndim == 1 else pltpu.VMEM)(a.shape, a.dtype) for a in operands] + [edge, edge],
        scratch_shapes=[pltpu.SemaphoreType.DMA((depth * (rows // TILE) + len(small),))],
        compiler_params=SMALL,
        name="load",
    )(*[pltpu.with_memory_space_constraint(a, pltpu.HBM) for a in operands])
    return outs[:-2], outs[-2], outs[-1]


def range_matrix(margin, rows, kernel_ref, index_row, offset_row, order, column):
    taps = kernel_ref.shape[0]
    both = taps_and_offsets(kernel_ref[...], index_row, offset_row, order)
    base = column + both[taps : taps + 1].astype(jnp.int32) + (margin - 3)
    place = iota((taps, order.shape[1]), 0) - base
    value = tap_pattern(both, place & (taps - 1))
    blocks = [jnp.where(over(place + start, taps) == 0, value, 0.0) for start in range(0, rows, taps)]
    return jnp.concatenate(blocks, 0)


def tap_pattern(both, which):
    value = jnp.zeros(which.shape, F32)
    for tap in range(both.shape[0] - 8):
        value = jnp.where(which == tap, both[tap : tap + 1], value)
    return value


def azimuth_kernel(
    margin, calls, x_ref, azk_ref, rgk_ref, rgo_ref, rgi_ref, azi_ref, azo_ref, z_ref, band_ref, *refs
):
    *rg_refs, spread_ref = refs
    depth, _, _, columns = x_ref.shape
    taps = azk_ref.shape[0]
    tile, lanes = spread_ref.shape
    half_rows, half_lanes = tile // 2, lanes // 2
    period = 2 * taps
    lane = iota((1, lanes), 1)
    row, part = lane_row(lane, half_rows)
    spread_ref[...] = chosen((tile, lanes), 0, row + half_rows * over(lane, half_lanes))
    column = look_column(iota((1, columns), 1), columns)
    order = chosen((columns, columns), 0, column)
    for rg_ref in rg_refs:
        for k in range(depth):
            rg_ref[k] = range_matrix(
                margin, columns + 2 * margin, rgk_ref, rgi_ref[k : k + 1], rgo_ref[k : k + 1], order, column
            ).astype(BF)
    for call, (k, chunk) in enumerate(calls):
        for s in range(2):
            start = (2 * chunk + s) * tile
            rows = slice(start, start + tile)
            both = taps_and_offsets(
                azk_ref[...], azi_ref[k : k + 1, rows], azo_ref[k : k + 1, rows], spread_ref[...]
            )
            base = row + both[taps : taps + 1].astype(jnp.int32) + (margin - 3)
            sub = iota((period, lanes), 0)
            place = (sub >> 1) - base
            value = tap_pattern(both, jnp.where((sub & 1) == part, place & (taps - 1), taps))
            home = -over(place, taps)
            for half in range(2):
                mine = slice(half * half_lanes, (half + 1) * half_lanes)
                band = band_ref.at[call, s, half]
                for block in range(band.shape[0] // period):
                    band[block * period : (block + 1) * period] = jnp.where(
                        home[:, mine] == block, value[:, mine], 0.0
                    ).astype(BF)
                begin = start + half * half_rows
                size = half_rows + 2 * margin
                window = x_ref[k, begin : begin + size].reshape(2 * size, columns)
                z_ref[call, s, half] = dot(window, band[...], OVER_ROWS).astype(BF)


def azimuth(operands, margin, calls, matrices):
    depth, _, parts, columns = operands[0].shape
    lanes = parts * TILE // 2
    shapes = [
        (len(calls), 2, 2, columns, lanes),
        (len(calls), 2, 2, parts * (TILE // 2 + 2 * margin), lanes),
    ]
    if matrices:
        shapes.append((depth, columns + 2 * margin, columns))
    return pl.pallas_call(
        partial(azimuth_kernel, margin, calls),
        in_specs=[VMEM] * len(operands),
        out_specs=[VMEM] * len(shapes),
        out_shape=[pltpu.VMEM(shape, BF) for shape in shapes],
        scratch_shapes=[pltpu.VMEM((TILE, parts * TILE), BF)],
        compiler_params=SMALL,
        name="azimuth",
    )(*resident(*operands))


def range_kernel(calls, z_ref, band_ref, rg_ref, first_ref, second_ref, *outs):
    odd_column = lax.axis_index("range") & 1 == 1
    half_rows = z_ref.shape[4] // 2
    for call, (out, (k, chunk)) in enumerate(zip(outs, calls)):
        for s in range(2):
            for half in range(2):
                at = (call, s, half)
                begin = 2 * (2 * (2 * chunk + s) + half) * half_rows
                across = slice(begin, begin + band_ref.shape[3])
                first_side, second_side = first_ref[k, :, across], second_ref[k, :, across]
                wide = jnp.concatenate(
                    [
                        dot(jnp.where(odd_column, first_side, second_side), band_ref[at]).astype(BF),
                        z_ref[at],
                        dot(jnp.where(odd_column, second_side, first_side), band_ref[at]).astype(BF),
                    ],
                    0,
                )
                out[s, half] = dot(rg_ref[k], wide, OVER_ROWS).astype(BF)


def range_resample(azimuth_outs, first, second, calls):
    _, _, _, columns, lanes = azimuth_outs[0].shape
    arrays = resident(*azimuth_outs, first, second)
    return pl.pallas_call(
        partial(range_kernel, calls),
        in_specs=[VMEM] * len(arrays),
        out_specs=[VMEM] * len(calls),
        out_shape=[pltpu.VMEM((2, 2, columns, lanes), BF)] * len(calls),
        compiler_params=SMALL,
        name="range_resample",
    )(*arrays)


def choose_kernel(bit, owner_ref, here_ref, there_ref, out_ref, sems):
    me = lax.axis_index("scene")
    copies = []
    for n in range(out_ref.shape[0]):
        tile = 2 * n + (me & 1)
        here, there = [ref.at[0, tile] if len(ref.shape) > 4 else ref.at[n] for ref in (here_ref, there_ref)]
        same = ((owner_ref[tile] ^ me) >> bit) & 1 == 0
        copies.append(pltpu.make_async_copy(here, out_ref.at[n], sems.at[n]))
        pl.when(same)(copies[n].start)
        pl.when(jnp.logical_not(same))(pltpu.make_async_copy(there, out_ref.at[n], sems.at[n]).start)
    for copy in copies:
        copy.wait()


def choose(owner, here, there, bit, chunks):
    return pl.pallas_call(
        partial(choose_kernel, bit),
        in_specs=[SMEM, VMEM, VMEM],
        out_specs=VMEM,
        out_shape=pltpu.VMEM((chunks, *here.shape[-3:]), BF),
        scratch_shapes=[pltpu.SemaphoreType.DMA((chunks,))],
        compiler_params=SMALL,
        name="choose",
    )(owner, *resident(here, there))


def lines(ref, look):
    blocks, width = ref.shape[0] // LOOK_RG, ref.shape[1] // 2
    wide = ref[look * blocks : (look + 1) * blocks].astype(F32)
    return wide[:, :width], wide[:, width:]


def multilook(terms, *refs):
    totals = None
    for look in range(LOOK_RG):
        found = terms(*[lines(ref, look) for ref in refs])
        totals = found if totals is None else [a + b for a, b in zip(totals, found)]
    means = []
    for total in totals:
        shift = total.shape[1] // 2
        while shift >= total.shape[1] // LOOK_AZ:
            total = total + pltpu.roll(total, shift, 1)
            shift //= 2
        means.append(total * (1.0 / (LOOK_AZ * LOOK_RG)))
    return means


def pair(first, second):
    a_re, a_im = first
    b_re, b_im = second
    return [a_re * b_re + a_im * b_im, a_im * b_re - a_re * b_im]


def power(first):
    re, im = first
    return [re * re + im * im]


def joined(pieces):
    blocks = pieces[0].shape[1] // LOOK_AZ
    group = over(iota(pieces[0].shape, 1), blocks)
    total = pieces[0]
    for position in range(1, len(pieces)):
        total = jnp.where(group >= position, pieces[position], total)
    return total


def gathered(units):
    return [joined(list(pieces)) for pieces in zip(*units)]


def reference_kernel(chunk, own_ref, mate_ref, *refs):
    depth = len(refs) - 3
    cur_refs, (pair_ref, pow_ref, lead_ref) = refs[:depth], refs[depth:]
    columns, half_rows = own_ref.shape[3], own_ref.shape[1] // 2
    core = lax.axis_index("scene") & 1
    size = 2 * half_rows
    row, part = lane_row(iota((1, size), 1), half_rows)
    order = chosen((size, size), 0, 2 * row + part)
    turn = chosen((columns, columns), 1, look_column(iota((columns, 1), 0), columns))

    def terms(lead, *currents):
        return power(lead) + [a for current in currents for a in pair(lead, current)]

    units = []
    for n, (ref, place) in enumerate(((own_ref, core), (mate_ref, 1 - core))):
        for half in range(2):
            rows = ref[chunk, half * half_rows : (half + 1) * half_rows].reshape(size, columns)
            lead_ref[2 * n + half] = dot(turn, dot(rows, order, OVER_ROWS).astype(BF)).astype(BF)
            units.append(
                multilook(terms, lead_ref.at[2 * n + half], *[ref.at[place, half] for ref in cur_refs])
            )
    units = [[jnp.where(core == 0, a, b) for a, b in zip(units[n], units[(n + 2) % 4])] for n in range(4)]
    pow_ref[...], *pairs = gathered(units)
    for n, found in enumerate(pairs):
        pair_ref[n // 2, n % 2] = found


def reference_products(own, mate, currents, chunk):
    _, _, columns, width = currents[0].shape
    depth = len(currents)
    shapes = [(depth, 2, columns // LOOK_RG, width // 2), (columns // LOOK_RG, width // 2)]
    return pl.pallas_call(
        partial(reference_kernel, chunk),
        in_specs=[VMEM] * (2 + depth),
        out_specs=[VMEM] * len(shapes),
        out_shape=[pltpu.VMEM(shape, F32) for shape in shapes],
        scratch_shapes=[pltpu.VMEM((4, columns, width), BF)],
        compiler_params=SMALL,
        name="reference_products",
    )(*resident(own, mate, *currents))


def units_of(ref):
    return [ref.at[n // 2, n % 2] for n in range(4)]


def within_kernel(depth, *refs):
    chunks = len(refs) // (depth + 4)

    def terms(*rows):
        return [a for row in rows for a in power(row)] + [
            a for k in range(len(rows) - 1) for a in pair(rows[k], rows[k + 1])
        ]

    for n in range(chunks):
        sources = refs[n * (depth + 1) : (n + 1) * (depth + 1)]
        lead_ref, seq_ref, pow_ref = refs[chunks * (depth + 1) + 3 * n :][:3]
        units = [multilook(terms, *unit) for unit in zip(*map(units_of, sources))]
        lead_ref[2], *found = gathered(units)
        for k in range(depth):
            pow_ref[k] = found[k]
        lead_ref[0], lead_ref[1], *pairs = found[depth:]
        for m, a in enumerate(pairs):
            seq_ref[m // 2, m % 2] = a


def within_products(got, currents):
    chunks, depth = len(currents), len(currents[0])
    _, _, columns, width = got[0].shape
    size = (columns // LOOK_RG, width // 2)
    arrays = [a for g, chunk in zip(got, currents) for a in (g, *chunk)]
    shapes = [(3, *size), (max(depth - 1, 1), 2, *size), (depth, *size)] * chunks
    outs = pl.pallas_call(
        partial(within_kernel, depth),
        in_specs=[VMEM] * len(arrays),
        out_specs=[VMEM] * len(shapes),
        out_shape=[pltpu.VMEM(shape, F32) for shape in shapes],
        compiler_params=SMALL,
        name="within_products",
    )(*resident(*arrays))
    return [outs[3 * n : 3 * n + 3] for n in range(chunks)]


def across_kernel(got_ref, first_ref, last_ref, out_ref):
    def products(leads, followers):
        units = [
            multilook(lambda a, b: pair(a, b) + power(a), *unit)
            for unit in zip(units_of(leads), units_of(followers))
        ]
        out_ref[0], out_ref[1], out_ref[2] = gathered(units)

    odd = lax.axis_index("scene") & 1 == 1
    pl.when(odd)(lambda: products(last_ref, got_ref))
    pl.when(jnp.logical_not(odd))(lambda: products(got_ref, first_ref))


def across_products(got, first, last):
    _, _, columns, width = got.shape
    return pl.pallas_call(
        across_kernel,
        in_specs=[VMEM] * 3,
        out_specs=VMEM,
        out_shape=pltpu.VMEM((3, columns // LOOK_RG, width // 2), F32),
        compiler_params=SMALL,
        name="across_products",
    )(*resident(got, first, last))


def pick_kernel(odd_ref, even_ref, out_ref):
    out_ref[...] = jnp.where(lax.axis_index("scene") & 1 == 1, odd_ref[...], even_ref[...])


def pick(odd, even):
    return pl.pallas_call(
        pick_kernel,
        in_specs=[VMEM] * 2,
        out_specs=VMEM,
        out_shape=pltpu.VMEM(odd.shape, odd.dtype),
        compiler_params=SMALL,
        name="pick",
    )(*resident(odd, even))


def finish_kernel(*refs):
    inputs, (ref_out, seq_out, coh_out) = refs[:-3], refs[-3:]
    at_head, odd = lax.axis_index("scene") == 0, lax.axis_index("scene") & 1 == 1
    lanes = inputs[1].shape[-1]
    for chunk in range(len(inputs) // 6):
        pairs, pair_pow, across, within, seq, powers = inputs[6 * chunk : 6 * chunk + 6]
        rows = slice(chunk * lanes, (chunk + 1) * lanes)

        def lead(place, own):
            return jnp.where(at_head, own, jnp.where(odd, within[place], across[place]))

        earlier = lead(2, pair_pow[...])
        for k in range(ref_out.shape[0]):
            if k:
                re, im = seq[k - 1, 0], seq[k - 1, 1]
            else:
                re, im = (lead(place, pairs[0, place]) for place in range(2))
            now = powers[k]
            ref_out[k, 0, :, rows] = pairs[k, 0]
            ref_out[k, 1, :, rows] = pairs[k, 1]
            seq_out[k, 0, :, rows] = re
            seq_out[k, 1, :, rows] = im
            coh_out[k, :, rows] = jnp.sqrt(re * re + im * im) / jnp.sqrt(earlier * now + eps_power)
            earlier = now


def finish(results, depth):
    flat = [a for result in results for a in result]
    blocks, lanes = flat[1].shape
    rows = len(results) * lanes
    shapes = [(depth, 2, blocks, rows)] * 2 + [(depth, blocks, rows)]
    outs = pl.pallas_call(
        finish_kernel,
        in_specs=[VMEM] * len(flat),
        out_specs=[VMEM] * 3,
        out_shape=[jax.ShapeDtypeStruct(shape, F32) for shape in shapes],
        compiler_params=SMALL,
        name="finish",
    )(*resident(*flat))
    return tuple(jnp.swapaxes(a, -1, -2) for a in outs)


def swapped(block, axis, bit):
    return lax.ppermute(block, axis, [(i, i ^ (1 << bit)) for i in range(lax.axis_size(axis))])


def neighbours(block, axis, first, around=False):
    count = lax.axis_size(axis)
    pairs = [(i, (i + 1) % count) for i in range(first, count - 1 + around, 2)]
    return lax.ppermute(block, axis, pairs + [(j, i) for i, j in pairs])


def local(
    secondary,
    reference_store,
    tile_owner,
    az_kernel,
    rg_kernel,
    az_offset,
    az_index,
    rg_offset,
    rg_index,
):
    depth = secondary.shape[0]
    chunks = reference_store.shape[1] // 2
    bits = lax.axis_size("scene").bit_length() - 1

    arrived = swapped(reference_store, "scene", 0)
    operands, first, second = load(
        secondary, tile_owner, reference_store, az_kernel.T, rg_kernel.T, rg_offset, rg_index, az_index, az_offset
    )
    secondary, owner, stored, *tables = operands
    operands = (secondary, *tables)
    owner = pltpu.with_memory_space_constraint(owner, pltpu.SMEM)
    held = choose(owner, stored, arrived, 0, chunks)
    for bit in range(1, bits):
        got = swapped(held, "scene", bit)
        held = choose(owner, held, got, bit, chunks)
    mate = swapped(held, "scene", 0)
    first = neighbours(first, "range", 0)
    second = neighbours(second, "range", 1)
    last = depth - 1
    early, late = [(last, 0), (0, 1)], [(k, n) for n in range(2) for k in range(depth)]
    late = [call for call in late if call not in early]
    *turned, matrices = azimuth(operands, first.shape[1], early, True)
    units = dict(zip(early, range_resample((*turned, matrices), first, second, early)))
    across = pick(units[last, 0], units[0, 1])
    across = neighbours(across, "scene", 1)
    turned = azimuth(operands, first.shape[1], late, False)
    units.update(zip(late, range_resample((*turned, matrices), first, second, late)))
    currents = [[units[k, n] for k in range(depth)] for n in range(2)]
    within = []
    for n in range(2):
        within.append(swapped(currents[n][last], "scene", 0))
    for n in range(2):
        within[n] = within_products([within[n]], [currents[n]])[0]
    across = across_products(across, currents[0][0], currents[1][last])
    returned = neighbours(across, "scene", 1, True)
    results = []
    for n, small in enumerate(within):
        pairs, pair_pow = reference_products(held, mate, currents[n], n)
        results.append((pairs, pair_pow, (across, returned)[n], *small))
    return finish(results, depth)


def solution(mesh):
    in_specs = (
        P(("parts", "scene"), None, None, "range"),
        P(("parts", "scene"), None, None, None, "range"),
        P("parts"),
        P(),
        P(),
        P(("parts", "scene"), None),
        P(("parts", "scene"), None),
        P(("parts", "scene"), "range"),
        P(("parts", "scene"), "range"),
    )
    out_specs = (
        P(("parts", "scene"), None, None, "range"),
        P(("parts", "scene"), None, None, "range"),
        P(("parts", "scene"), None, "range"),
    )
    return jax.shard_map(local, mesh=mesh, in_specs=in_specs, out_specs=out_specs, check_vma=False)
```

```python
from functools import partial

import jax
import jax.numpy as jnp
from jax import lax
from jax.experimental import pallas as pl
from jax.experimental.pallas import tpu as pltpu
from jax.sharding import PartitionSpec as P


TILE = 256
LOOK_AZ = 4
LOOK_RG = 16

eps_power = 1e-06

BF = jnp.bfloat16
F32 = jnp.float32
ACROSS = (((1,), (0,)), ((), ()))
OVER_ROWS = (((0,), (0,)), ((), ()))
OVER_LANES = (((1,), (1,)), ((), ()))
VMEM = pl.BlockSpec(memory_space=pltpu.VMEM)
SMEM = pl.BlockSpec(memory_space=pltpu.SMEM)
SMALL = pltpu.CompilerParams(vmem_limit_bytes=12 << 20)


def iota(shape, dim):
    return lax.broadcasted_iota(jnp.int32, shape, dim)


def over(value, size):
    return value >> (size.bit_length() - 1)


def dot(a, b, dims=ACROSS):
    return lax.dot_general(a, b, dims, preferred_element_type=F32)


def lane_row(lane, half_rows):
    blocks = half_rows // LOOK_AZ
    inner = lane & (half_rows - 1)
    return LOOK_AZ * (inner & (blocks - 1)) + over(inner, blocks), over(lane, half_rows) & 1


def look_column(place, columns):
    blocks = columns // LOOK_RG
    return LOOK_RG * (place & (blocks - 1)) + over(place, blocks)


def chosen(shape, dim, wanted):
    return (iota(shape, dim) == wanted).astype(F32).astype(BF)


def taps_and_offsets(kernel_t, index_row, offset_row, spread):
    count = kernel_t.shape[1]
    taps = dot(kernel_t.astype(BF), chosen((count, index_row.shape[1]), 0, index_row))
    offsets = jnp.broadcast_to(offset_row.astype(F32), (8, offset_row.shape[1]))
    return dot(jnp.concatenate([taps, offsets], 0).astype(BF), spread)


def resident(*arrays):
    return [pltpu.with_memory_space_constraint(a, pltpu.VMEM) for a in arrays]


def load_kernel(margin, x_ref, *refs):
    count = (len(refs) - 4) // 2
    small_refs, x_out, outs = refs[:count], refs[count], refs[count + 1 : 2 * count + 1]
    first_ref, second_ref, sems = refs[2 * count + 1 :]
    depth, rows, parts, columns = x_ref.shape
    step = 2 * TILE
    pieces = [(k, n) for k in range(depth) for n in range(rows // step)]

    def copy_of(position):
        k, n = pieces[position]
        size = step if n + 1 < rows // step else rows - n * step
        part = (k, pl.ds(n * step, size))
        return pltpu.make_async_copy(x_ref.at[part], x_out.at[part], sems.at[position]), part, size

    copies = [copy_of(position) for position in range(len(pieces))]
    small = [
        pltpu.make_async_copy(source, target, sems.at[len(pieces) + n])
        for n, (source, target) in enumerate(zip(small_refs, outs))
    ]
    for copy, _, _ in copies:
        copy.start()
    for copy in small:
        copy.start()
    place = iota((2 * margin, 1), 0)
    right_first = place + jnp.where(place < margin, columns - margin, -margin)
    left_first = place + jnp.where(place < margin, 0, columns - 2 * margin)
    edges = chosen((2 * margin, columns), 1, jnp.where(lax.axis_index("range") & 1 == 0, right_first, left_first))
    for (k, n), (copy, part, size) in zip(pieces, copies):
        copy.wait()
        found = dot(edges, x_out[part].reshape(parts * size, columns), OVER_LANES).astype(BF)
        lanes = slice(parts * n * step, parts * (n * step + size))
        first_ref[k, :, lanes] = found[:margin]
        second_ref[k, :, lanes] = found[margin:]
    for copy in small:
        copy.wait()


def load(secondary, *small):
    depth, rows, parts, _ = secondary.shape
    margin = (rows - small[-1].shape[1]) // 2
    operands = (secondary, *small)
    edge = pltpu.VMEM((depth, margin, parts * rows), BF)
    anywhere = pl.BlockSpec(memory_space=pl.ANY)
    outs = pl.pallas_call(
        partial(load_kernel, margin),
        in_specs=[anywhere] * len(operands),
        out_specs=[SMEM if a.ndim == 1 else VMEM for a in operands] + [VMEM] * 2,
        out_shape=[(pltpu.SMEM if a.ndim == 1 else pltpu.VMEM)(a.shape, a.dtype) for a in operands] + [edge, edge],
        scratch_shapes=[pltpu.SemaphoreType.DMA((depth * (rows // TILE) + len(small),))],
        compiler_params=SMALL,
        name="load",
    )(*[pltpu.with_memory_space_constraint(a, pltpu.HBM) for a in operands])
    return outs[:-2], outs[-2], outs[-1]


def range_matrix(margin, rows, kernel_ref, index_row, offset_row, order, column):
    taps = kernel_ref.shape[0]
    both = taps_and_offsets(kernel_ref[...], index_row, offset_row, order)
    base = column + both[taps : taps + 1].astype(jnp.int32) + (margin - 3)
    place = iota((taps, order.shape[1]), 0) - base
    value = tap_pattern(both, place & (taps - 1))
    blocks = [jnp.where(over(place + start, taps) == 0, value, 0.0) for start in range(0, rows, taps)]
    return jnp.concatenate(blocks, 0)


def tap_pattern(both, which):
    value = jnp.zeros(which.shape, F32)
    for tap in range(both.shape[0] - 8):
        value = jnp.where(which == tap, both[tap : tap + 1], value)
    return value


def azimuth_kernel(
    margin, calls, x_ref, azk_ref, rgk_ref, rgo_ref, rgi_ref, azi_ref, azo_ref, z_ref, band_ref, *refs
):
    *rg_refs, spread_ref = refs
    depth, _, _, columns = x_ref.shape
    taps = azk_ref.shape[0]
    tile, lanes = spread_ref.shape
    half_rows, half_lanes = tile // 2, lanes // 2
    period = 2 * taps
    lane = iota((1, lanes), 1)
    row, part = lane_row(lane, half_rows)
    spread_ref[...] = chosen((tile, lanes), 0, row + half_rows * over(lane, half_lanes))
    column = look_column(iota((1, columns), 1), columns)
    order = chosen((columns, columns), 0, column)
    for rg_ref in rg_refs:
        for k in range(depth):
            rg_ref[k] = range_matrix(
                margin, columns + 2 * margin, rgk_ref, rgi_ref[k : k + 1], rgo_ref[k : k + 1], order, column
            ).astype(BF)
    for call, (k, chunk) in enumerate(calls):
        for s in range(2):
            start = (2 * chunk + s) * tile
            rows = slice(start, start + tile)
            both = taps_and_offsets(
                azk_ref[...], azi_ref[k : k + 1, rows], azo_ref[k : k + 1, rows], spread_ref[...]
            )
            base = row + both[taps : taps + 1].astype(jnp.int32) + (margin - 3)
            sub = iota((period, lanes), 0)
            place = (sub >> 1) - base
            value = tap_pattern(both, jnp.where((sub & 1) == part, place & (taps - 1), taps))
            home = -over(place, taps)
            for half in range(2):
                mine = slice(half * half_lanes, (half + 1) * half_lanes)
                band = band_ref.at[call, s, half]
                for block in range(band.shape[0] // period):
                    band[block * period : (block + 1) * period] = jnp.where(
                        home[:, mine] == block, value[:, mine], 0.0
                    ).astype(BF)
                begin = start + half * half_rows
                size = half_rows + 2 * margin
                window = x_ref[k, begin : begin + size].reshape(2 * size, columns)
                z_ref[call, s, half] = dot(window, band[...], OVER_ROWS).astype(BF)


def azimuth(operands, margin, calls, matrices):
    depth, _, parts, columns = operands[0].shape
    lanes = parts * TILE // 2
    shapes = [
        (len(calls), 2, 2, columns, lanes),
        (len(calls), 2, 2, parts * (TILE // 2 + 2 * margin), lanes),
    ]
    if matrices:
        shapes.append((depth, columns + 2 * margin, columns))
    return pl.pallas_call(
        partial(azimuth_kernel, margin, calls),
        in_specs=[VMEM] * len(operands),
        out_specs=[VMEM] * len(shapes),
        out_shape=[pltpu.VMEM(shape, BF) for shape in shapes],
        scratch_shapes=[pltpu.VMEM((TILE, parts * TILE), BF)],
        compiler_params=SMALL,
        name="azimuth",
    )(*resident(*operands))


def range_kernel(calls, z_ref, band_ref, rg_ref, first_ref, second_ref, *outs):
    odd_column = lax.axis_index("range") & 1 == 1
    half_rows = z_ref.shape[4] // 2
    for call, (out, (k, chunk)) in enumerate(zip(outs, calls)):
        for s in range(2):
            for half in range(2):
                at = (call, s, half)
                begin = 2 * (2 * (2 * chunk + s) + half) * half_rows
                across = slice(begin, begin + band_ref.shape[3])
                first_side, second_side = first_ref[k, :, across], second_ref[k, :, across]
                wide = jnp.concatenate(
                    [
                        dot(jnp.where(odd_column, first_side, second_side), band_ref[at]).astype(BF),
                        z_ref[at],
                        dot(jnp.where(odd_column, second_side, first_side), band_ref[at]).astype(BF),
                    ],
                    0,
                )
                out[s, half] = dot(rg_ref[k], wide, OVER_ROWS).astype(BF)


def range_resample(azimuth_outs, first, second, calls):
    _, _, _, columns, lanes = azimuth_outs[0].shape
    arrays = resident(*azimuth_outs, first, second)
    return pl.pallas_call(
        partial(range_kernel, calls),
        in_specs=[VMEM] * len(arrays),
        out_specs=[VMEM] * len(calls),
        out_shape=[pltpu.VMEM((2, 2, columns, lanes), BF)] * len(calls),
        compiler_params=SMALL,
        name="range_resample",
    )(*arrays)


def choose_kernel(bit, owner_ref, here_ref, there_ref, out_ref, sems):
    me = lax.axis_index("scene")
    copies = []
    for n in range(out_ref.shape[0]):
        tile = 2 * n + (me & 1)
        here, there = [ref.at[0, tile] if len(ref.shape) > 4 else ref.at[n] for ref in (here_ref, there_ref)]
        same = ((owner_ref[tile] ^ me) >> bit) & 1 == 0
        copies.append(pltpu.make_async_copy(here, out_ref.at[n], sems.at[n]))
        pl.when(same)(copies[n].start)
        pl.when(jnp.logical_not(same))(pltpu.make_async_copy(there, out_ref.at[n], sems.at[n]).start)
    for copy in copies:
        copy.wait()


def choose(owner, here, there, bit, chunks):
    return pl.pallas_call(
        partial(choose_kernel, bit),
        in_specs=[SMEM, VMEM, VMEM],
        out_specs=VMEM,
        out_shape=pltpu.VMEM((chunks, *here.shape[-3:]), BF),
        scratch_shapes=[pltpu.SemaphoreType.DMA((chunks,))],
        compiler_params=SMALL,
        name="choose",
    )(owner, *resident(here, there))


def lines(ref, look):
    blocks, width = ref.shape[0] // LOOK_RG, ref.shape[1] // 2
    wide = ref[look * blocks : (look + 1) * blocks].astype(F32)
    return wide[:, :width], wide[:, width:]


def multilook(terms, *refs):
    totals = None
    for look in range(LOOK_RG):
        found = terms(*[lines(ref, look) for ref in refs])
        totals = found if totals is None else [a + b for a, b in zip(totals, found)]
    means = []
    for total in totals:
        shift = total.shape[1] // 2
        while shift >= total.shape[1] // LOOK_AZ:
            total = total + pltpu.roll(total, shift, 1)
            shift //= 2
        means.append(total * (1.0 / (LOOK_AZ * LOOK_RG)))
    return means


def pair(first, second):
    a_re, a_im = first
    b_re, b_im = second
    return [a_re * b_re + a_im * b_im, a_im * b_re - a_re * b_im]


def power(first):
    re, im = first
    return [re * re + im * im]


def joined(pieces):
    blocks = pieces[0].shape[1] // LOOK_AZ
    group = over(iota(pieces[0].shape, 1), blocks)
    total = pieces[0]
    for position in range(1, len(pieces)):
        total = jnp.where(group >= position, pieces[position], total)
    return total


def gathered(units):
    return [joined(list(pieces)) for pieces in zip(*units)]


def reference_kernel(chunk, own_ref, mate_ref, *refs):
    depth = len(refs) - 3
    cur_refs, (pair_ref, pow_ref, lead_ref) = refs[:depth], refs[depth:]
    columns, half_rows = own_ref.shape[3], own_ref.shape[1] // 2
    core = lax.axis_index("scene") & 1
    size = 2 * half_rows
    row, part = lane_row(iota((1, size), 1), half_rows)
    order = chosen((size, size), 0, 2 * row + part)
    turn = chosen((columns, columns), 1, look_column(iota((columns, 1), 0), columns))

    def terms(lead, *currents):
        return power(lead) + [a for current in currents for a in pair(lead, current)]

    units = []
    for n, (ref, place) in enumerate(((own_ref, core), (mate_ref, 1 - core))):
        for half in range(2):
            rows = ref[chunk, half * half_rows : (half + 1) * half_rows].reshape(size, columns)
            lead_ref[2 * n + half] = dot(turn, dot(rows, order, OVER_ROWS).astype(BF)).astype(BF)
            units.append(
                multilook(terms, lead_ref.at[2 * n + half], *[ref.at[place, half] for ref in cur_refs])
            )
    units = [[jnp.where(core == 0, a, b) for a, b in zip(units[n], units[(n + 2) % 4])] for n in range(4)]
    pow_ref[...], *pairs = gathered(units)
    for n, found in enumerate(pairs):
        pair_ref[n // 2, n % 2] = found


def reference_products(own, mate, currents, chunk):
    _, _, columns, width = currents[0].shape
    depth = len(currents)
    shapes = [(depth, 2, columns // LOOK_RG, width // 2), (columns // LOOK_RG, width // 2)]
    return pl.pallas_call(
        partial(reference_kernel, chunk),
        in_specs=[VMEM] * (2 + depth),
        out_specs=[VMEM] * len(shapes),
        out_shape=[pltpu.VMEM(shape, F32) for shape in shapes],
        scratch_shapes=[pltpu.VMEM((4, columns, width), BF)],
        compiler_params=SMALL,
        name="reference_products",
    )(*resident(own, mate, *currents))


def units_of(ref):
    return [ref.at[n // 2, n % 2] for n in range(4)]


def within_kernel(depth, *refs):
    chunks = len(refs) // (depth + 4)

    def terms(*rows):
        return [a for row in rows for a in power(row)] + [
            a for k in range(len(rows) - 1) for a in pair(rows[k], rows[k + 1])
        ]

    for n in range(chunks):
        sources = refs[n * (depth + 1) : (n + 1) * (depth + 1)]
        lead_ref, seq_ref, pow_ref = refs[chunks * (depth + 1) + 3 * n :][:3]
        units = [multilook(terms, *unit) for unit in zip(*map(units_of, sources))]
        lead_ref[2], *found = gathered(units)
        for k in range(depth):
            pow_ref[k] = found[k]
        lead_ref[0], lead_ref[1], *pairs = found[depth:]
        for m, a in enumerate(pairs):
            seq_ref[m // 2, m % 2] = a


def within_products(got, currents):
    chunks, depth = len(currents), len(currents[0])
    _, _, columns, width = got[0].shape
    size = (columns // LOOK_RG, width // 2)
    arrays = [a for g, chunk in zip(got, currents) for a in (g, *chunk)]
    shapes = [(3, *size), (max(depth - 1, 1), 2, *size), (depth, *size)] * chunks
    outs = pl.pallas_call(
        partial(within_kernel, depth),
        in_specs=[VMEM] * len(arrays),
        out_specs=[VMEM] * len(shapes),
        out_shape=[pltpu.VMEM(shape, F32) for shape in shapes],
        compiler_params=SMALL,
        name="within_products",
    )(*resident(*arrays))
    return [outs[3 * n : 3 * n + 3] for n in range(chunks)]


def across_kernel(got_ref, first_ref, last_ref, out_ref):
    def products(leads, followers):
        units = [
            multilook(lambda a, b: pair(a, b) + power(a), *unit)
            for unit in zip(units_of(leads), units_of(followers))
        ]
        out_ref[0], out_ref[1], out_ref[2] = gathered(units)

    odd = lax.axis_index("scene") & 1 == 1
    pl.when(odd)(lambda: products(last_ref, got_ref))
    pl.when(jnp.logical_not(odd))(lambda: products(got_ref, first_ref))


def across_products(got, first, last):
    _, _, columns, width = got.shape
    return pl.pallas_call(
        across_kernel,
        in_specs=[VMEM] * 3,
        out_specs=VMEM,
        out_shape=pltpu.VMEM((3, columns // LOOK_RG, width // 2), F32),
        compiler_params=SMALL,
        name="across_products",
    )(*resident(got, first, last))


def pick_kernel(odd_ref, even_ref, out_ref):
    out_ref[...] = jnp.where(lax.axis_index("scene") & 1 == 1, odd_ref[...], even_ref[...])


def pick(odd, even):
    return pl.pallas_call(
        pick_kernel,
        in_specs=[VMEM] * 2,
        out_specs=VMEM,
        out_shape=pltpu.VMEM(odd.shape, odd.dtype),
        compiler_params=SMALL,
        name="pick",
    )(*resident(odd, even))


def finish_kernel(*refs):
    inputs, (ref_out, seq_out, coh_out) = refs[:-3], refs[-3:]
    at_head, odd = lax.axis_index("scene") == 0, lax.axis_index("scene") & 1 == 1
    lanes = inputs[1].shape[-1]
    for chunk in range(len(inputs) // 6):
        pairs, pair_pow, across, within, seq, powers = inputs[6 * chunk : 6 * chunk + 6]
        rows = slice(chunk * lanes, (chunk + 1) * lanes)

        def lead(place, own):
            return jnp.where(at_head, own, jnp.where(odd, within[place], across[place]))

        earlier = lead(2, pair_pow[...])
        for k in range(ref_out.shape[0]):
            if k:
                re, im = seq[k - 1, 0], seq[k - 1, 1]
            else:
                re, im = (lead(place, pairs[0, place]) for place in range(2))
            now = powers[k]
            ref_out[k, 0, :, rows] = pairs[k, 0]
            ref_out[k, 1, :, rows] = pairs[k, 1]
            seq_out[k, 0, :, rows] = re
            seq_out[k, 1, :, rows] = im
            coh_out[k, :, rows] = jnp.sqrt(re * re + im * im) / jnp.sqrt(earlier * now + eps_power)
            earlier = now


def finish(results, depth):
    flat = [a for result in results for a in result]
    blocks, lanes = flat[1].shape
    rows = len(results) * lanes
    shapes = [(depth, 2, blocks, rows)] * 2 + [(depth, blocks, rows)]
    outs = pl.pallas_call(
        finish_kernel,
        in_specs=[VMEM] * len(flat),
        out_specs=[VMEM] * 3,
        out_shape=[jax.ShapeDtypeStruct(shape, F32) for shape in shapes],
        compiler_params=SMALL,
        name="finish",
    )(*resident(*flat))
    return tuple(jnp.swapaxes(a, -1, -2) for a in outs)


def swapped(block, axis, bit):
    return lax.ppermute(block, axis, [(i, i ^ (1 << bit)) for i in range(lax.axis_size(axis))])


def neighbours(block, axis, first, around=False):
    count = lax.axis_size(axis)
    pairs = [(i, (i + 1) % count) for i in range(first, count - 1 + around, 2)]
    return lax.ppermute(block, axis, pairs + [(j, i) for i, j in pairs])


def local(
    secondary,
    reference_store,
    tile_owner,
    az_kernel,
    rg_kernel,
    az_offset,
    az_index,
    rg_offset,
    rg_index,
):
    depth = secondary.shape[0]
    chunks = reference_store.shape[1] // 2
    bits = lax.axis_size("scene").bit_length() - 1

    arrived = swapped(reference_store, "scene", 0)
    operands, first, second = load(
        secondary, tile_owner, reference_store, az_kernel.T, rg_kernel.T, rg_offset, rg_index, az_index, az_offset
    )
    secondary, owner, stored, *tables = operands
    operands = (secondary, *tables)
    owner = pltpu.with_memory_space_constraint(owner, pltpu.SMEM)
    held = choose(owner, stored, arrived, 0, chunks)
    for bit in range(1, bits):
        got = swapped(held, "scene", bit)
        held = choose(owner, held, got, bit, chunks)
    mate = swapped(held, "scene", 0)
    first = neighbours(first, "range", 0)
    second = neighbours(second, "range", 1)
    last = depth - 1
    early, late = [(last, 0), (0, 1)], [(k, n) for n in range(2) for k in range(depth)]
    late = [call for call in late if call not in early]
    *turned, matrices = azimuth(operands, first.shape[1], early, True)
    units = dict(zip(early, range_resample((*turned, matrices), first, second, early)))
    across = pick(units[last, 0], units[0, 1])
    across = neighbours(across, "scene", 1)
    turned = azimuth(operands, first.shape[1], late, False)
    units.update(zip(late, range_resample((*turned, matrices), first, second, late)))
    currents = [[units[k, n] for k in range(depth)] for n in range(2)]
    within = []
    for n in range(2):
        within.append(swapped(currents[n][last], "scene", 0))
    for n in range(2):
        within[n] = within_products([within[n]], [currents[n]])[0]
    across = across_products(across, currents[0][0], currents[1][last])
    returned = neighbours(across, "scene", 1, True)
    results = []
    for n, small in enumerate(within):
        pairs, pair_pow = reference_products(held, mate, currents[n], n)
        results.append((pairs, pair_pow, (across, returned)[n], *small))
    return finish(results, depth)


def solution(mesh):
    in_specs = (
        P(("parts", "scene"), None, None, "range"),
        P(("parts", "scene"), None, None, None, "range"),
        P("parts"),
        P(),
        P(),
        P(("parts", "scene"), None),
        P(("parts", "scene"), None),
        P(("parts", "scene"), "range"),
        P(("parts", "scene"), "range"),
    )
    out_specs = (
        P(("parts", "scene"), None, None, "range"),
        P(("parts", "scene"), None, None, "range"),
        P(("parts", "scene"), None, "range"),
    )
    return jax.shard_map(local, mesh=mesh, in_specs=in_specs, out_specs=out_specs, check_vma=False)
```
